32 devices in a mesh: parts: 2 (over y), req: 4 (over z), tp: 2 (over x), sp: 2 (over core).
Axes of the slice: x: 2, y: 2, z: 4, core: 2. Of those that a mesh axis runs over, the one named last changes fastest.
Arguments:
- prompt_x: bfloat16 [1024, 16384], P(('parts', 'req', 'sp'), 'tp'), parts along dimension 0, may hold values from -600 to 600
- prompt_b: bfloat16 [1024, 8, 128], P(('parts', 'req', 'sp'), 'tp'), parts along dimension 0, may hold values from -0.5 to 0.5
- prompt_dt: float32 [1024, 256], P(('parts', 'req', 'sp'), 'tp'), parts along dimension 0, may hold values from 0.5 to 2
- cont_x: bfloat16 [8, 256, 16384], P(('parts', 'req'), 'sp', 'tp'), parts along dimension 0, may hold values from -6 to 6
- cont_bc: bfloat16 [8, 256, 2, 8, 128], P(('parts', 'req'), 'sp', None, 'tp'), parts along dimension 0, may hold values from -0.5 to 0.5
- cont_dt: float32 [8, 256, 256], P(('parts', 'req'), 'sp', 'tp'), parts along dimension 0, may hold values from 0.5 to 2
- decay_rate: float32 [256], P('tp'), may hold values from 0.0063476562 to 0.05
- skip_gain: float32 [256], P('tp'), may hold values from 0.5 to 1.5
- norm_gain: float32 [16384], P('tp'), may hold values from 0.25 to 1.75
- steer_vecs: float32 [7, 16384], P(None, 'tp'), may hold values from -3 to 3
- mult_table: float32 [9], replicated, may hold values from -3 to 3
- mult_idx: int32 [8], P(('parts', 'req')), parts along dimension 0, may hold values from 0 to 8
- behav_idx: int32 [8], P(('parts', 'req')), parts along dimension 0, may hold values from 0 to 6
Outputs:
- steered_out: bfloat16 [8, 256, 16384], P(('parts', 'req'), 'sp', 'tp'), parts along dimension 0
The draws below stay inside these ranges and needn't reach their ends.
There are 2 independent parts, one for each index of `parts`. The reference program is written for one: setup_inputs(seed, part) draws one part's arguments, and reference() takes and returns one part's arrays. A program takes and returns all parts, laid end to end along the dimension named above; an argument that names none is the same for every part. Nothing has to cross between parts.
All inputs are finite; a program needn't handle non-finite values.
Results may differ from the reference program's by a relative error of at most 0.008.
Values sent between devices are 32-bit elements; how exact they have to be, the bound alone decides.
A program may use at most 320 MiB of HBM per device.

```python
import math
import jax
import jax.numpy as jnp
from jax import lax

HEADS = 256
HEAD_DIM = 64
GROUPS = 8
STATE = 128
BEHAV = 7
NMULT = 9
PRE_DEV = 64
CONT_DEV = 128
PROMPT = 512
CONT = 256
REQS = 4
N_SP = 2


def draw_prompt_x(key, part):
    distance = (PROMPT - 1 - jnp.arange(PROMPT, dtype=jnp.float32)) / PROMPT
    ramp = jnp.exp(5.0 * distance)[:, None]
    values = jax.random.truncated_normal(key, -4.0, 4.0, (PROMPT, HEADS * HEAD_DIM), jnp.float32)
    return (values * ramp).astype(jnp.bfloat16)


def draw_decay_rate(key, part):
    pick_key, slow_key, fast_key = jax.random.split(key, 3)
    slow = jnp.exp(jax.random.uniform(slow_key, (HEADS,), jnp.float32, jnp.log(3.25), jnp.log(5.55))) / PROMPT
    fast = jnp.exp(jax.random.uniform(fast_key, (HEADS,), jnp.float32, jnp.log(0.02), jnp.log(0.05)))
    quick = jax.random.bernoulli(pick_key, 0.25, (HEADS,))
    return jnp.where(quick, fast, slow)


def place_ends(values, own_key, least, high):
    extent = values.shape
    spot = [jax.random.randint(jax.random.fold_in(own_key, axis), (), 0, extent[axis]) for axis in range(len(extent))]
    values = values.at[tuple(spot)].set(least)
    longest = extent.index(max(extent))
    spot[longest] = (spot[longest] + 1) % extent[longest]
    return values.at[tuple(spot)].set(high)


def shard_levels(own_key, extent, cuts, smallest, high):
    def one(dim, shards_of):
        steps = jax.random.uniform(jax.random.fold_in(jax.random.fold_in(own_key, 6), dim), (shards_of,), jnp.float32, smallest / len(cuts), high / len(cuts))
        return jnp.repeat(jnp.exp(steps), extent[dim] // shards_of).reshape((-1,) + (1,) * (len(extent) - dim - 1))

    level = one(*cuts[0])
    for cut in cuts[1:]:
        level = level * one(*cut)
    return level


def bell_draw(stream_key, extent, deviation, reach, shards=(), kind=jnp.bfloat16):
    result = deviation * jax.random.normal(stream_key, extent, jnp.float32)
    if shards:
        result = result * shard_levels(stream_key, extent, shards, -0.22, 0.18)
    return jnp.clip(result, -reach, reach).astype(kind)


def setup_inputs(seed: int = 0, part: int = 0) -> dict:
    seeds = jax.random.split(jax.random.key(seed), 14)
    own_keys = jax.random.split(jax.random.fold_in(seeds[13], part), 14)
    return {
        "prompt_x": draw_prompt_x(jax.random.fold_in(jax.random.fold_in(seeds[13], part), 71), part),
        "prompt_b": bell_draw(own_keys[1], (PROMPT, GROUPS, STATE), STATE ** -0.5, 0.5, ((0, 8), (1, 2))),
        "prompt_dt": jnp.clip(jnp.exp(math.log(2.0) - 1.3862944 * jax.random.uniform(own_keys[2], (PROMPT, HEADS), jnp.float32) ** shard_levels(own_keys[2], (PROMPT, HEADS), ((0, 8), (1, 2)), -0.2, 0.2)), 0.5, 2.0),
        "cont_x": bell_draw(own_keys[3], (REQS, CONT, HEADS * HEAD_DIM), 1.0, 6.0, ((0, 4), (1, 2), (2, 2))),
        "cont_bc": bell_draw(own_keys[4], (REQS, CONT, 2, GROUPS, STATE), STATE ** -0.5, 0.5, ((0, 4), (1, 2), (3, 2))),
        "cont_dt": jnp.clip(jnp.exp(math.log(2.0) - 1.3862944 * jax.random.uniform(own_keys[5], (REQS, CONT, HEADS), jnp.float32) ** shard_levels(own_keys[5], (REQS, CONT, HEADS), ((0, 4), (1, 2), (2, 2)), -0.2, 0.2)), 0.5, 2.0),
        "decay_rate": draw_decay_rate(jax.random.fold_in(seeds[13], 71), part),
        "skip_gain": jnp.clip(0.5 + 1.0 * jax.random.uniform(seeds[7], (HEADS,), jnp.float32) ** shard_levels(seeds[7], (HEADS,), ((0, 2),), -0.2, 0.2), 0.5, 1.5),
        "norm_gain": jnp.clip(1.0 + 0.15 * jax.random.normal(seeds[8], (HEADS * HEAD_DIM,), jnp.float32), 0.25, 1.75),
        "steer_vecs": bell_draw(seeds[9], (BEHAV, HEADS * HEAD_DIM), 0.5, 3.0, ((1, 2),), jnp.float32),
        "mult_table": jnp.clip(jax.random.uniform(seeds[10], (NMULT,), jnp.float32, -3.0, 3.0), -3.0, 3.0),
        "mult_idx": place_ends(jax.random.randint(own_keys[11], (REQS,), 0, NMULT), jax.random.fold_in(own_keys[11], 1), 0, NMULT - 1).astype(jnp.int32),
        "behav_idx": place_ends(jax.random.randint(own_keys[12], (REQS,), 0, BEHAV), jax.random.fold_in(own_keys[12], 1), 0, BEHAV - 1).astype(jnp.int32),
    }


def block_state(rows_x, rows_b, rows_dt, decay_rate, groups):
    length = rows_x.shape[0]
    head_count = decay_rate.shape[0]
    per_group = head_count // groups
    head_size = rows_x.shape[1] // head_count
    cumulative = jnp.cumsum(-decay_rate[None, :] * rows_dt, axis=0)
    block_total = cumulative[-1]
    weight = jnp.exp(block_total[None, :] - cumulative) * rows_dt
    scaled = (rows_x.astype(jnp.float32).reshape(length, head_count, head_size) * weight[:, :, None]).astype(jnp.bfloat16)
    scaled = scaled.reshape(length, groups, per_group, head_size)
    local_state = jnp.einsum('tgqp,tgn->gqpn', scaled.astype(jnp.float32), rows_b.astype(jnp.float32), precision=lax.Precision.HIGHEST)
    carried = jnp.einsum('tgq,tgn->gqn', weight.reshape(length, groups, per_group), rows_b.astype(jnp.float32), precision=lax.Precision.HIGHEST)
    return (block_total, local_state.reshape(head_count, head_size, -1), carried.reshape(head_count, -1), cumulative)

def intra_block(steered, bmat, cmat, rows_dt, cumulative, groups):
    length = steered.shape[0]
    head_count = rows_dt.shape[1]
    per_group = head_count // groups
    head_size = steered.shape[1] // head_count
    products = jnp.einsum('tgn,sgn->gts', cmat.astype(jnp.float32), bmat.astype(jnp.float32), precision=lax.Precision.HIGHEST)
    lower_mask = lax.broadcasted_iota(jnp.int32, (length, length), 0) >= lax.broadcasted_iota(jnp.int32, (length, length), 1)
    cum_groups = cumulative.reshape(length, groups, per_group).transpose(1, 2, 0)
    step_groups = rows_dt.reshape(length, groups, per_group).transpose(1, 2, 0)
    input_groups = steered.reshape(length, groups, per_group, head_size).transpose(1, 0, 2, 3)

    def one_group(pieces):
        product_one, cum_one, step_one, input_one = pieces
        differ = cum_one[:, :, None] - cum_one[:, None, :]
        decays = jnp.exp(jnp.where(lower_mask[None], differ, -1e+30))
        mixing = (decays * step_one[:, None, :] * product_one[None]).astype(jnp.bfloat16)
        return jnp.einsum('qts,sqp->tqp', mixing.astype(jnp.float32), input_one.astype(jnp.float32), precision=lax.Precision.HIGHEST)
    outputs = lax.map(one_group, (products, cum_groups, step_groups, input_groups))
    return outputs.transpose(1, 0, 2, 3).reshape(length, head_count, head_size)

def reference(prompt_x, prompt_b, prompt_dt, cont_x, cont_bc, cont_dt, decay_rate, skip_gain, norm_gain, steer_vecs, mult_table, mult_idx, behav_idx):
    blocks = PROMPT // PRE_DEV
    width = HEADS * HEAD_DIM
    per_group = HEADS // GROUPS

    def prompt_step(carry_pair, pieces):
        block_x, block_b, block_dt = pieces
        block_total, local_state, carried, cumulative = block_state(block_x, block_b, block_dt, decay_rate, GROUPS)
        decay_all = jnp.exp(block_total)
        return ((decay_all[:, None, None] * carry_pair[0] + local_state, decay_all[:, None] * carry_pair[1] + carried), None)
    zeros_pair = (jnp.zeros((HEADS, HEAD_DIM, STATE), jnp.float32), jnp.zeros((HEADS, STATE), jnp.float32))
    (prefix_state, prefix_carry), unused = lax.scan(prompt_step, zeros_pair, (prompt_x.reshape(blocks, PRE_DEV, width), prompt_b.reshape(blocks, PRE_DEV, GROUPS, STATE), prompt_dt.reshape(blocks, PRE_DEV, HEADS)))

    def one_request(pieces):
        request_x, request_bc, request_dt, mult_one, behav_one = pieces
        multiplier = mult_table[mult_one]
        vector = steer_vecs[behav_one]
        steered = (request_x.astype(jnp.float32) + multiplier * vector[None, :]).astype(jnp.bfloat16)
        incoming = prefix_state + multiplier * vector.reshape(HEADS, HEAD_DIM)[:, :, None] * prefix_carry[:, None, :]
        results = []
        for block_index in range(N_SP):
            first = block_index * CONT_DEV
            rows_x = steered[first:first + CONT_DEV]
            bmat = request_bc[first:first + CONT_DEV, 0]
            cmat = request_bc[first:first + CONT_DEV, 1]
            rows_dt = request_dt[first:first + CONT_DEV]
            block_total, local_state, carried, cumulative = block_state(rows_x, bmat, rows_dt, decay_rate, GROUPS)
            inner = intra_block(rows_x, bmat, cmat, rows_dt, cumulative, GROUPS)
            incoming_round = incoming.astype(jnp.bfloat16).reshape(GROUPS, per_group, HEAD_DIM, STATE)
            from_state = jnp.einsum('tgn,gqpn->tgqp', cmat.astype(jnp.float32), incoming_round.astype(jnp.float32), precision=lax.Precision.HIGHEST).reshape(CONT_DEV, HEADS, HEAD_DIM)
            skipped = skip_gain[None, :, None] * rows_x.astype(jnp.float32).reshape(CONT_DEV, HEADS, HEAD_DIM)
            results.append(inner + jnp.exp(cumulative)[:, :, None] * from_state + skipped)
            incoming = jnp.exp(block_total)[:, None, None] * incoming + local_state
        mixed = jnp.concatenate(results, axis=0).reshape(CONT, width)
        meansq = lax.optimization_barrier(jnp.sum(mixed * mixed, axis=1)) / (HEADS * HEAD_DIM)
        return (mixed * lax.rsqrt(meansq + 1e-05)[:, None] * norm_gain[None, :]).astype(jnp.bfloat16)
    return lax.map(one_request, (cont_x, cont_bc, cont_dt, mult_idx, behav_idx))
```

```python
import functools

import jax
import jax.numpy as jnp
from jax import lax
from jax.experimental import pallas as pl
from jax.experimental.pallas import tpu as pltpu
from jax.sharding import PartitionSpec as P

MESH = pl.DeviceIdType.MESH
F32 = jnp.float32
BF16 = jnp.bfloat16
LANES = 128
WIDTH = 128
PAIR = 2
QUAD = 4
PIECE = 512
AHEAD = 4
SKEW = 3
LAG = 1
LATE = 4


def dot(a, b):
    return jnp.dot(a, b, preferred_element_type=F32)


def dot_t(a, b):
    return lax.dot_general(a, b, (((1,), (1,)), ((), ())), preferred_element_type=F32)


def thirds(value):
    lead = value.astype(BF16)
    rest = value - lead.astype(F32)
    mid = rest.astype(BF16)
    low = (rest - mid.astype(F32)).astype(BF16)
    return jnp.concatenate([lead, mid, low], axis=0)


def running_sum(rows):
    length = rows.shape[0]
    lower = lax.broadcasted_iota(jnp.int32, (length, length), 0) >= lax.broadcasted_iota(
        jnp.int32, (length, length), 1
    )
    ones = jnp.where(lower, 1.0, 0.0).astype(BF16)
    return dot(jnp.concatenate([ones] * 3, axis=1), thirds(rows))


def kernel(
    R,
    TP,
    K,
    HP,
    px,
    pb,
    pdt,
    cx,
    cbc,
    cdt,
    rate,
    skip,
    gain,
    vecs,
    table,
    mult_at,
    behav_at,
    out,
    scale_out,
    pdv,
    pbv,
    rav,
    skv,
    gav,
    tav,
    pxv,
    cxv,
    cbv,
    cdv,
    vev,
    pxs,
    pxr,
    us,
    ur,
    pbs,
    pbr,
    pbt,
    w2,
    colw,
    roww,
    gc,
    cbt,
    mv,
    skc,
    fc,
    tots,
    ctot,
    ctot_in,
    sc,
    st0,
    s_own,
    s_lin,
    s_lout,
    s_rin,
    s_rout,
    s_tot,
    s_ag,
    c_own,
    c_lin,
    c_lout,
    c_rin,
    c_rout,
    c_tot,
    c_ag,
    carw,
    ssacc,
    ssl,
    h_sem,
    t_send,
    t_recv,
    x_send,
    x_recv,
    l_send,
    l_recv,
    r_send,
    r_recv,
    a_send,
    a_recv,
    z_send,
    z_recv,
    d_send,
    d_recv,
    p_send,
    p_recv,
):
    i = lax.axis_index("req")
    s = lax.axis_index("sp")
    x = lax.axis_index("tp")
    me = i * 2 + s
    other = i * 2 + 1 - s
    hr = R - 1 - i
    far = jnp.maximum(i, hr)
    tok, H = pdt.shape
    block = WIDTH * PAIR
    wide_block = WIDTH * QUAD

    C = px.shape[1]
    Gd, N = pb.shape[1:]
    T = cx.shape[0]
    half = C // 2
    head = C // H
    gw = C // Gd
    per_group = H // Gd
    nh = N // 2
    NX = half // PIECE
    PER = PIECE // WIDTH
    sib = {"sp": 1 - s}
    first, last = i == 0, i == R - 1

    def each(count, skip_index, body):
        def turn(j, carry):
            @pl.when(j != skip_index)
            def _():
                body(j)

            return carry

        lax.fori_loop(0, count, turn, 0)

    def peer(j):
        return {"req": j // 2, "sp": j % 2}

    def remote(src, dst, send, recv, device):
        return pltpu.make_async_remote_copy(
            src_ref=src,
            dst_ref=dst,
            send_sem=send,
            recv_sem=recv,
            device_id=device,
            device_id_type=MESH,
        )

    def h_copy(src, dst, k):
        return pltpu.make_async_copy(src, dst, h_sem.at[k])

    def piece_at(owner, q):
        return pl.ds(pl.multiple_of(owner * half + q * PIECE, PIECE), PIECE)

    own_half = pl.ds(pl.multiple_of(s * half, half), half)
    pieces = [
        h_copy(px.at[:, piece_at(1 - s, q)], pxv.at[:, piece_at(1 - s, q)], q) for q in range(NX)
    ]
    early = [
        h_copy(pdt, pdv, NX),
        h_copy(rate, rav, NX + 1),
        h_copy(pb, pbv, NX + 2),
    ]
    px_own = h_copy(px.at[:, own_half], pxv.at[:, own_half], NX + 3)
    cdt_in = h_copy(cdt, cdv, NX + 4)
    cbc_in = h_copy(cbc, cbv, NX + 5)
    later = [
        h_copy(vecs, vev, NX + 6),
        h_copy(table, tav, NX + 7),
        h_copy(skip, skv, NX + 8),
        h_copy(gain, gav, NX + 9),
    ]
    cx_in = h_copy(cx, cxv, NX + 10)
    barrier = pltpu.get_barrier_semaphore()

    def greet(j, carry):
        @pl.when((j > me) | (j == other) | (j == me - 2))
        def _():
            pl.semaphore_signal(barrier, inc=1, device_id=peer(j), device_id_type=MESH)

        return carry

    lax.fori_loop(0, 2 * R, greet, 0)
    each(
        TP,
        x,
        lambda j: pl.semaphore_signal(barrier, inc=1, device_id={"tp": j}, device_id_type=MESH),
    )
    for copy in early:
        copy.start()
    for copy in pieces:
        copy.start()
    for copy in [px_own, cdt_in, cbc_in] + later + [cx_in]:
        copy.start()

    for copy in early:
        copy.wait()
    cum = running_sum(-rav[...] * pdv[...])
    total = cum[tok - 1 :, :]
    tots[me] = jnp.broadcast_to(total, (8, H))
    us[...] = jnp.exp(total - cum) * pdv[...]
    for g in range(Gd):
        pbs[g] = pbv[:, g, :].astype(F32)
    pieces[0].wait()
    pxs[0] = pxv[:, piece_at(1 - s, 0)].astype(F32)
    greeted = me + (1 - s) + jnp.where(i < R - 1, 1, 0) + TP - 1
    pl.semaphore_wait(barrier, greeted)

    def tot_copy(j, slot):
        return remote(tots.at[slot], tots.at[slot], t_send.at[j], t_recv.at[slot], peer(j))

    def x_copy(src, dst, k):
        return remote(src, dst, x_send.at[k], x_recv.at[k], sib)

    def px_x(q):
        return x_copy(pxs.at[q], pxr.at[q], q)

    def u_x():
        return x_copy(us, ur, NX)

    def pb_x():
        return x_copy(pbs, pbr, NX + 1)

    def d_copy():
        return remote(ctot, ctot_in, d_send.at[0], d_recv.at[0], sib)

    u_x().start()
    pb_x().start()
    px_x(0).start()

    def tell(j, carry):
        tot_copy(j, me).start()
        return carry

    lax.fori_loop(0, me, tell, 0)

    for q in range(1, NX):
        pieces[q].wait()
        pxs[q] = pxv[:, piece_at(1 - s, q)].astype(F32)
        px_x(q).start()

    def padded(value):
        return jnp.concatenate([value] * (HP // H), axis=1) if HP > H else value

    def spread(value, base, width):
        lane = lax.broadcasted_iota(jnp.int32, (value.shape[0], LANES), 1)
        shift = head.bit_length() - 1
        parts = []
        for q in range(width // LANES):
            at = lax.shift_right_logical(lane, shift) + (base // head + q * (LANES // head))
            parts.append(jnp.take_along_axis(value, at, axis=1, mode="promise_in_bounds"))
        return parts[0] if len(parts) == 1 else jnp.concatenate(parts, axis=1)

    def place(owner, k):
        return pl.multiple_of(owner * half + k * WIDTH, WIDTH)

    u_x().wait_recv()
    pb_x().wait_recv()
    for g in range(Gd):
        pbt[g] = jnp.concatenate([pbs[g], pbr[g]], axis=0).T.astype(BF16)
    px_own.wait()

    def heard(j, carry):
        tot_copy(j, j).wait_recv()
        return carry

    lax.fori_loop(me + 1, 2 * R, heard, 0)

    slot = lax.broadcasted_iota(jnp.int32, tots.shape, 0)
    every = tots[...]
    after_me = jnp.sum(jnp.where(slot > me, every, 0.0), axis=0)[0:1, :]
    after_other = jnp.sum(jnp.where(slot > other, every, 0.0), axis=0)[0:1, :]
    w2[:tok, :H] = us[...] * jnp.exp(after_me)
    w2[tok:, :H] = ur[...] * jnp.exp(after_other)

    def produce(k):
        base = place(s, k)

        @pl.when(k % PER == 0)
        def _():
            px_x(k // PER).wait_recv()

        at = pl.ds(pl.multiple_of((k % PER) * WIDTH, WIDTH), block)
        mine = pxv[:, pl.ds(base, block)].astype(F32) * spread(w2[:tok], base, block)
        theirs = pxr[k // PER, :, at] * spread(w2[tok:], base, block)
        scaled = jnp.concatenate([mine, theirs], axis=0).astype(BF16)
        state = dot(pbt[base // gw], scaled)
        for q in range(PAIR):
            s_own[k + q] = state[:, q * WIDTH : (q + 1) * WIDTH]

    def l_copy(src, dst, k):
        return remote(src, dst, l_send.at[k], l_recv.at[k], {"req": jnp.minimum(i + 1, R - 1)})

    def r_copy(src, dst, k):
        return remote(src, dst, r_send.at[k], r_recv.at[k], {"req": jnp.maximum(i - 1, 0)})

    def state_l(k):
        return l_copy(s_lout.at[k], s_lin.at[k], k)

    def own_l(k):
        return l_copy(s_own.at[k], s_lin.at[k], k)

    def state_r(k):
        return r_copy(s_rout.at[k], s_rin.at[k], k)

    def own_r(k):
        return r_copy(s_own.at[k], s_rin.at[k], k)

    def carry_l():
        return l_copy(c_lout, c_lin, K)

    def own_carry_l():
        return l_copy(c_own, c_lin, K)

    def carry_r():
        return r_copy(c_rout, c_rin, K)

    def own_carry_r():
        return r_copy(c_own, c_rin, K)

    def carry_a():
        return remote(c_tot, c_ag, a_send.at[K], a_recv.at[K], sib)

    def state_a(k):
        return remote(s_tot.at[k], s_ag.at[k], a_send.at[k], a_recv.at[k], sib)

    def z_copy(j):
        rows = pl.ds(j * QUAD, QUAD)
        return remote(st0.at[rows], st0.at[rows], z_send.at[j], z_recv.at[j], sib)

    def push(source, sink, own, came, out_ref, relay, straight):
        @pl.when(source)
        def _():
            straight().start()

        @pl.when(jnp.logical_not(source))
        def _():
            relay().wait_recv()

            @pl.when(jnp.logical_not(sink))
            def _():
                out_ref[...] = own[...] + came[...]
                relay().start()

    def close(own, lin, lout, rin, tot, copy):
        @pl.when(first)
        def _():
            tot[...] = own[...] + rin[...]

        @pl.when(last)
        def _():
            tot[...] = own[...] + lin[...]

        @pl.when(jnp.logical_not(first | last))
        def _():
            tot[...] = lout[...] + rin[...]

        copy().start()

    def cont_chunk(owner, k):
        base = place(owner, k)
        j = owner * K + k
        at = pl.ds(base, wide_block)
        steered = (cxv[:, at].astype(F32) + mv[:, at]).astype(BF16)
        wide = steered.astype(F32)
        out[:, at] = skc[0:1, at] * wide
        scaled = (wide * spread(colw[...], base, wide_block)).astype(BF16)
        for q in range(QUAD):
            sc[j + q] = scaled[:, q * WIDTH : (q + 1) * WIDTH]

        @pl.when(s == 0)
        def _():
            state = dot(cbt[base // gw], scaled)
            for q in range(QUAD):
                st0[j + q] = state[:, q * WIDTH : (q + 1) * WIDTH]
            z_copy(j // QUAD).start()

    def finish(owner, k, ready):
        base = place(owner, k)
        j = owner * K + k
        at = pl.ds(base, block)
        coming = jnp.concatenate([ready[k + q] for q in range(PAIR)], axis=1)
        before = jnp.concatenate([st0[j + q] for q in range(PAIR)], axis=1)
        start = coming + spread(carw[...], base, block) * mv[:, at]
        incoming = ((start + second * before) * fc[0:1, at]).astype(BF16)
        scaled = jnp.concatenate([sc[j + q] for q in range(PAIR)], axis=1)
        z = dot(gc[base // gw], jnp.concatenate([scaled, incoming], axis=0))
        mixed = out[:, at] + spread(roww[...], base, block) * z
        out[:, at] = mixed * gav[:, at]
        square = mixed * mixed
        folded = square[:, :LANES]
        for q in range(1, block // LANES):
            folded = folded + square[:, q * LANES : (q + 1) * LANES]
        return folded

    def sent(k):
        state_a(k).wait_send()

        @pl.when(jnp.logical_not(last))
        def _():
            state_l(k).wait_send()

        @pl.when(jnp.logical_not(first))
        def _():
            state_r(k).wait_send()

        @pl.when((s == 0) & (k % QUAD == 0))
        def _():
            z_copy(k // QUAD).wait_send()
            z_copy((k + K) // QUAD).wait_send()

    def within(k):
        return (k >= 0) & (k < K)

    second = jnp.where(s == 1, 1.0, 0.0).astype(F32)
    produce(jnp.int32(0))

    @pl.when(first)
    def _():
        own_l(0).start()

    @pl.when(last)
    def _():
        own_r(0).start()

    lane_group = lax.broadcasted_iota(jnp.int32, (nh, H), 1)
    carry = jnp.zeros((nh, H), F32)
    weight = thirds(w2[:, :H])
    rows = pl.ds(pl.multiple_of(s * nh, nh), nh)
    for g in range(Gd):
        inside = (lane_group >= g * per_group) & (lane_group < (g + 1) * per_group)
        part = dot(jnp.concatenate([pbt[g, rows]] * 3, axis=1), weight)
        carry = jnp.where(inside, part, carry)
    c_own[...] = carry

    for k in range(PAIR, AHEAD, PAIR):
        produce(jnp.int32(k))
    cdt_in.wait()
    ccum = running_sum(-rav[...] * cdv[...])
    ctot[...] = jnp.broadcast_to(ccum[T - 1 :, :], (8, H))

    @pl.when(s == 0)
    def _():
        d_copy().start()

    colw[:, :H] = jnp.exp(-ccum) * cdv[...]
    roww[:, :H] = jnp.exp(ccum)
    ssacc[...] = jnp.zeros_like(ssacc)
    for copy in later:
        copy.wait()
    entry = lax.broadcasted_iota(jnp.int32, tav.shape, 1) == mult_at[0]
    multiplier = jnp.sum(jnp.where(entry, tav[...], 0.0), axis=1, keepdims=True)
    wanted = lax.broadcasted_iota(jnp.int32, vecs.shape, 0) == behav_at[0]
    mv[...] = multiplier * jnp.sum(jnp.where(wanted, vev[...], 0.0), axis=0, keepdims=True)
    cbc_in.wait()
    lower = lax.broadcasted_iota(jnp.int32, (T, T), 0) >= lax.broadcasted_iota(
        jnp.int32, (T, T), 1
    )
    for g in range(Gd):
        bmat = cbv[:, 0, g, :].astype(F32)
        cmat = cbv[:, 1, g, :].astype(F32).astype(BF16)
        cbt[g] = bmat.T.astype(BF16)
        gmat = jnp.where(lower, dot_t(cmat, bmat.astype(BF16)), 0.0)
        gc[g] = jnp.concatenate([gmat.astype(BF16), cmat], axis=1)

    def row_of(value, to):
        value = padded(jnp.broadcast_to(value, (8, H)))
        lane = lax.broadcasted_iota(jnp.int32, (8, LANES), 1)
        for q in range(C // LANES):
            at = lax.shift_right_logical(lane, head.bit_length() - 1) + q * (LANES // head)
            to[:, q * LANES : (q + 1) * LANES] = jnp.take_along_axis(
                value, at, axis=1, mode="promise_in_bounds"
            )

    row_of(skv[...], skc)

    @pl.when(s == 0)
    def _():
        fc[...] = jnp.ones_like(fc)

    @pl.when(s == 1)
    def _():
        d_copy().wait_recv()
        row_of(jnp.exp(ctot_in[0:1, :]), fc)

    cx_in.wait()

    def step(m, unused):
        kl = m - SKEW * i
        kr = m - SKEW * hr
        kt = m - SKEW * far
        kf = kt - LAG
        ks = kf - LATE

        @pl.when(within(kl) & (kl + i > 0))
        def _():
            push(
                first,
                last,
                s_own.at[kl],
                s_lin.at[kl],
                s_lout.at[kl],
                functools.partial(state_l, kl),
                functools.partial(own_l, kl),
            )

        @pl.when(within(kr) & (kr + hr > 0))
        def _():
            push(
                last,
                first,
                s_own.at[kr],
                s_rin.at[kr],
                s_rout.at[kr],
                functools.partial(state_r, kr),
                functools.partial(own_r, kr),
            )

        @pl.when(kl == 0)
        def _():
            push(first, last, c_own, c_lin, c_lout, carry_l, own_carry_l)

        @pl.when(kr == 0)
        def _():
            push(last, first, c_own, c_rin, c_rout, carry_r, own_carry_r)

        @pl.when(within(kt))
        def _():
            close(
                s_own.at[kt],
                s_lin.at[kt],
                s_lout.at[kt],
                s_rin.at[kt],
                s_tot.at[kt],
                functools.partial(state_a, kt),
            )

        @pl.when(kt == 0)
        def _():
            close(c_own, c_lin, c_lout, c_rin, c_tot, carry_a)

        @pl.when((m % PAIR == 0) & (m + AHEAD < K))
        def _():
            produce(m + AHEAD)

        @pl.when(m < 2 * K // QUAD)
        def _():
            cont_chunk(jnp.where(m % 2 == 0, s, 1 - s), m // 2 * QUAD)

        @pl.when(kf == 0)
        def _():
            carry_a().wait_recv()
            carw[pl.ds(pl.multiple_of(s * nh, nh), nh), :H] = c_tot[...]
            carw[pl.ds(pl.multiple_of((1 - s) * nh, nh), nh), :H] = c_ag[...]

        @pl.when(within(kf) & (kf % PAIR == PAIR - 1))
        def _():
            for q in range(PAIR):
                state_a(kf - q).wait_recv()

            @pl.when((s == 1) & (kf % QUAD == PAIR - 1))
            def _():
                z_copy(kf // QUAD).wait_recv()
                z_copy((kf + K) // QUAD).wait_recv()

            k = kf - PAIR + 1
            ssacc[...] += finish(s, k, s_tot) + finish(1 - s, k, s_ag)

        @pl.when(within(ks))
        def _():
            sent(ks)

        return unused

    steps = K + SKEW * (R - 1) + LAG
    lax.fori_loop(0, steps, step, 0)

    folded = ssacc[...].T
    partial = folded[0:8]
    for q in range(1, LANES // 8):
        partial = partial + folded[q * 8 : (q + 1) * 8]
    ssl[x] = partial

    def p_copy(j, at):
        return remote(ssl.at[at], ssl.at[at], p_send.at[j], p_recv.at[at], {"tp": j})

    each(TP, x, lambda j: p_copy(j, x).start())

    def left(k, unused):
        sent(k)
        return unused

    lowest = jnp.maximum(0, jnp.minimum(K, steps - SKEW * far - LAG - LATE))
    lax.fori_loop(lowest, K, left, 0)
    for q in range(NX):
        px_x(q).wait_send()
    u_x().wait_send()
    pb_x().wait_send()
    carry_a().wait_send()

    @pl.when(jnp.logical_not(last))
    def _():
        carry_l().wait_send()

    @pl.when(jnp.logical_not(first))
    def _():
        carry_r().wait_send()

    @pl.when(s == 0)
    def _():
        d_copy().wait_send()

    def told(j, carry):
        tot_copy(j, me).wait_send()
        return carry

    lax.fori_loop(0, me, told, 0)


    each(TP, x, lambda j: p_copy(j, j).wait_recv())
    meansq = jnp.sum(jnp.sum(ssl[...], axis=0), axis=0, keepdims=True) / (C * TP)
    scale_out[...] = jnp.broadcast_to(lax.rsqrt(meansq + 1e-05), scale_out.shape)
    each(TP, x, lambda j: p_copy(j, x).wait_send())


def local(
    prompt_x,
    prompt_b,
    prompt_dt,
    cont_x,
    cont_bc,
    cont_dt,
    decay_rate,
    skip_gain,
    norm_gain,
    steer_vecs,
    mult_table,
    mult_idx,
    behav_idx,
):
    R, TP = lax.axis_size("req"), lax.axis_size("tp")
    H = decay_rate.shape[0]
    tok, C = prompt_x.shape
    Gd, N = prompt_b.shape[1:]
    T = cont_x.shape[1]
    K = C // 2 // WIDTH
    NX = C // 2 // PIECE
    HP = max(H, LANES)
    def outside_of(*values):
        return tuple(pltpu.with_memory_space_constraint(v, pltpu.HBM) for v in values)

    args = outside_of(
        prompt_x,
        prompt_b,
        prompt_dt,
        cont_x[0],
        cont_bc[0],
        cont_dt[0],
        decay_rate[None],
        skip_gain[None],
        norm_gain[None],
        steer_vecs,
        mult_table[None],
    ) + (mult_idx, behav_idx)
    vmem, dma = pltpu.VMEM, pltpu.SemaphoreType.DMA
    inside = pl.BlockSpec(memory_space=pltpu.VMEM)
    outside = pl.BlockSpec(memory_space=pl.ANY)
    scalars = pl.BlockSpec(memory_space=pltpu.SMEM)
    part = (K, N, WIDTH)
    carried = (N // 2, H)
    scratch = (
        [
            vmem((tok, H), F32),
            vmem((tok, Gd, N), BF16),
            vmem((1, H), F32),
            vmem((1, H), F32),
            vmem((1, C), F32),
            vmem((1, mult_table.shape[0]), F32),
            vmem((tok, C), BF16),
            vmem((T, C), BF16),
            vmem(cont_bc.shape[1:], BF16),
            vmem((T, H), F32),
            vmem(steer_vecs.shape, F32),
        ]
        + [vmem((NX, tok, PIECE), F32)] * 2
        + [vmem((tok, H), F32)] * 2
        + [vmem((Gd, tok, N), F32)] * 2
        + [vmem((Gd, N, 2 * tok), BF16)]
        + [vmem((2 * tok, HP), F32)]
        + [vmem((T, HP), F32)] * 2
        + [vmem((Gd, T, T + N), BF16), vmem((Gd, N, T), BF16)]
        + [vmem((1, C), F32), vmem((8, C), F32), vmem((8, C), F32)]
        + [vmem((2 * R, 8, H), F32)]
        + [vmem((8, H), F32)] * 2
        + [vmem((2 * K, T, WIDTH), BF16)]
        + [vmem((2 * K, N, WIDTH), F32)]
        + [vmem(part, F32)] * 7
        + [vmem(carried, F32)] * 7
        + [vmem((N, HP), F32), vmem((T, LANES), F32), vmem((TP, 8, T), F32)]
        + [dma((NX + 11,))]
        + [dma((2 * R,))] * 2
        + [dma((NX + 2,))] * 2
        + [dma((K + 1,))] * 4
        + [dma((K + 1,))] * 2
        + [dma((2 * K // QUAD,))] * 2
        + [dma((1,))] * 2
        + [dma((TP,))] * 2
    )
    mixed, scale = pl.pallas_call(
        functools.partial(kernel, R, TP, K, HP),
        out_shape=[jax.ShapeDtypeStruct((T, C), F32), jax.ShapeDtypeStruct((8, T), F32)],
        in_specs=[outside] * 11 + [scalars] * 2,
        out_specs=[inside, inside],
        scratch_shapes=scratch,
        compiler_params=pltpu.CompilerParams(
            collective_id=0, has_side_effects=True, vmem_limit_bytes=40 * 1024 * 1024
        ),
        name="sweep",
    )(*args)
    return (mixed * scale[0][:, None]).astype(BF16)[None]


def solution(mesh):
    return jax.shard_map(
        local,
        mesh=mesh,
        in_specs=(
            P(("parts", "req", "sp"), "tp"),
            P(("parts", "req", "sp"), "tp", None),
            P(("parts", "req", "sp"), "tp"),
            P(("parts", "req"), "sp", "tp"),
            P(("parts", "req"), "sp", None, "tp", None),
            P(("parts", "req"), "sp", "tp"),
            P("tp"),
            P("tp"),
            P("tp"),
            P(None, "tp"),
            P(),
            P(("parts", "req")),
            P(("parts", "req")),
        ),
        out_specs=P(("parts", "req"), "sp", "tp"),
        check_vma=False,
    )
```

```python
import functools

import jax
import jax.numpy as jnp
from jax import lax
from jax.experimental import pallas as pl
from jax.experimental.pallas import tpu as pltpu
from jax.sharding import PartitionSpec as P

MESH = pl.DeviceIdType.MESH
F32 = jnp.float32
BF16 = jnp.bfloat16
LANES = 128
WIDTH = 128
PAIR = 2
QUAD = 4
OCT = 8
PIECE = 1024
RING = 4
AHEAD = 4
SKEW_L = 3
SKEW_R = 2
LAG = 1


def dot(a, b):
    return jnp.dot(a, b, preferred_element_type=F32)


def dot_t(a, b):
    return lax.dot_general(a, b, (((1,), (1,)), ((), ())), preferred_element_type=F32)


def thirds(value):
    lead = value.astype(BF16)
    rest = value - lead.astype(F32)
    mid = rest.astype(BF16)
    low = (rest - mid.astype(F32)).astype(BF16)
    return jnp.concatenate([lead, mid, low], axis=0)


def running_sum(rows):
    length = rows.shape[0]
    lower = lax.broadcasted_iota(jnp.int32, (length, length), 0) >= lax.broadcasted_iota(
        jnp.int32, (length, length), 1
    )
    ones = jnp.where(lower, 1.0, 0.0).astype(BF16)
    return dot(jnp.concatenate([ones] * 3, axis=1), thirds(rows))


def kernel(
    R,
    TP,
    K,
    HP,
    px,
    pb,
    pdt,
    cx,
    cbc,
    cdt,
    rate,
    skip,
    gain,
    vecs,
    table,
    mult_at,
    behav_at,
    out,
    scale_out,
    pdv,
    pbv,
    rav,
    skv,
    gav,
    tav,
    pxv,
    cxv,
    cbv,
    cdv,
    vev,
    pxs,
    pxr,
    us,
    ur,
    pbs,
    pbr,
    pbt,
    w2,
    colw,
    roww,
    gc,
    cbt,
    mv,
    skc,
    fc,
    tots,
    ctot,
    ctot_in,
    sc,
    st0,
    s_own,
    s_lin,
    s_lout,
    s_rin,
    s_rout,
    s_tot,
    s_ag,
    c_own,
    c_lin,
    c_lout,
    c_rin,
    c_rout,
    c_tot,
    c_ag,
    carw,
    ssacc,
    ssl,
    h_sem,
    t_send,
    t_recv,
    x_send,
    x_recv,
    l_send,
    l_recv,
    r_send,
    r_recv,
    a_send,
    a_recv,
    z_send,
    z_recv,
    d_send,
    d_recv,
    p_send,
    p_recv,
):
    i = lax.axis_index("req")
    s = lax.axis_index("sp")
    x = lax.axis_index("tp")
    me = i * 2 + s
    other = i * 2 + 1 - s
    hr = R - 1 - i
    far = jnp.maximum(SKEW_L * i, SKEW_R * hr)
    tok, H = pdt.shape
    block = WIDTH * PAIR
    wide_block = WIDTH * QUAD

    C = px.shape[1]
    Gd, N = pb.shape[1:]
    T = cx.shape[0]
    half = C // 2
    head = C // H
    gw = C // Gd
    per_group = H // Gd
    nh = N // 2
    NX = half // PIECE
    PER = PIECE // WIDTH
    sib = {"sp": 1 - s}
    first, last = i == 0, i == R - 1

    def each(count, skip_index, body):
        def turn(j, carry):
            @pl.when(j != skip_index)
            def _():
                body(j)

            return carry

        lax.fori_loop(0, count, turn, 0)

    def peer(j):
        return {"req": j // 2, "sp": j % 2}

    def remote(src, dst, send, recv, device):
        return pltpu.make_async_remote_copy(
            src_ref=src,
            dst_ref=dst,
            send_sem=send,
            recv_sem=recv,
            device_id=device,
            device_id_type=MESH,
        )

    def h_copy(src, dst, k):
        return pltpu.make_async_copy(src, dst, h_sem.at[k])

    def piece_at(owner, q):
        return pl.ds(pl.multiple_of(owner * half + q * PIECE, PIECE), PIECE)

    own_half = pl.ds(pl.multiple_of(s * half, half), half)
    pieces = [
        h_copy(px.at[:, piece_at(1 - s, q)], pxv.at[:, piece_at(1 - s, q)], q) for q in range(NX)
    ]
    early = [
        h_copy(pdt, pdv, NX),
        h_copy(rate, rav, NX + 1),
        h_copy(pb, pbv, NX + 2),
    ]
    px_own = h_copy(px.at[:, own_half], pxv.at[:, own_half], NX + 3)
    cdt_in = h_copy(cdt, cdv, NX + 4)
    cbc_in = h_copy(cbc, cbv, NX + 5)
    later = [
        h_copy(vecs, vev, NX + 6),
        h_copy(table, tav, NX + 7),
        h_copy(skip, skv, NX + 8),
        h_copy(gain, gav, NX + 9),
    ]
    cx_in = h_copy(cx, cxv, NX + 10)
    barrier = pltpu.get_barrier_semaphore()

    def greet(j, carry):
        @pl.when((j > me) | (j == other) | (j == me - 2))
        def _():
            pl.semaphore_signal(barrier, inc=1, device_id=peer(j), device_id_type=MESH)

        return carry

    lax.fori_loop(0, 2 * R, greet, 0)
    each(
        TP,
        x,
        lambda j: pl.semaphore_signal(barrier, inc=1, device_id={"tp": j}, device_id_type=MESH),
    )
    for copy in early:
        copy.start()
    for copy in pieces:
        copy.start()
    for copy in [px_own, cdt_in, cbc_in] + later + [cx_in]:
        copy.start()

    for copy in early:
        copy.wait()
    cum = running_sum(-rav[...] * pdv[...])
    total = cum[tok - 1 :, :]
    tots[me] = jnp.broadcast_to(total, (8, H))
    us[...] = jnp.exp(total - cum) * pdv[...]
    for g in range(Gd):
        pbs[g] = pbv[:, g, :].astype(F32)
    pieces[0].wait()
    pxs[0] = pxv[:, piece_at(1 - s, 0)].astype(F32)
    greeted = me + (1 - s) + jnp.where(i < R - 1, 1, 0) + TP - 1
    pl.semaphore_wait(barrier, greeted)

    def tot_copy(j, slot):
        return remote(tots.at[slot], tots.at[slot], t_send.at[j], t_recv.at[slot], peer(j))

    def x_copy(src, dst, up, k):
        return remote(src, dst, x_send.at[up], x_recv.at[k], sib)

    def px_x(q):
        return x_copy(pxs.at[q], pxr.at[q], 0, q)

    def u_x():
        return x_copy(us, ur, 1, NX)

    def pb_x():
        return x_copy(pbs, pbr, 2, NX + 1)

    def d_copy():
        return remote(ctot, ctot_in, d_send.at[0], d_recv.at[0], sib)

    u_x().start()
    pb_x().start()
    px_x(0).start()

    def tell(j, carry):
        tot_copy(j, me).start()
        return carry

    lax.fori_loop(0, me, tell, 0)

    for q in range(1, NX):
        pieces[q].wait()
        pxs[q] = pxv[:, piece_at(1 - s, q)].astype(F32)
        px_x(q).start()

    def padded(value):
        return jnp.concatenate([value] * (HP // H), axis=1) if HP > H else value

    def spread(value, base, width):
        lane = lax.broadcasted_iota(jnp.int32, (value.shape[0], LANES), 1)
        shift = head.bit_length() - 1
        parts = []
        for q in range(width // LANES):
            at = lax.shift_right_logical(lane, shift) + (base // head + q * (LANES // head))
            parts.append(jnp.take_along_axis(value, at, axis=1, mode="promise_in_bounds"))
        return parts[0] if len(parts) == 1 else jnp.concatenate(parts, axis=1)

    def place(owner, k):
        return pl.multiple_of(owner * half + k * WIDTH, WIDTH)

    u_x().wait_recv()
    pb_x().wait_recv()
    for g in range(Gd):
        pbt[g] = jnp.concatenate([pbs[g], pbr[g]], axis=0).T.astype(BF16)
    px_own.wait()

    def heard(j, carry):
        tot_copy(j, j).wait_recv()
        return carry

    lax.fori_loop(me + 1, 2 * R, heard, 0)

    slot = lax.broadcasted_iota(jnp.int32, tots.shape, 0)
    every = tots[...]
    after_me = jnp.sum(jnp.where(slot > me, every, 0.0), axis=0)[0:1, :]
    after_other = jnp.sum(jnp.where(slot > other, every, 0.0), axis=0)[0:1, :]
    w2[:tok, :H] = us[...] * jnp.exp(after_me)
    w2[tok:, :H] = ur[...] * jnp.exp(after_other)

    def produce(k):
        base = place(s, k)

        @pl.when(k % PER == 0)
        def _():
            px_x(k // PER).wait_recv()

        at = pl.ds(pl.multiple_of((k % PER) * WIDTH, WIDTH), block)
        mine = pxv[:, pl.ds(base, block)].astype(F32) * spread(w2[:tok], base, block)
        theirs = pxr[k // PER, :, at] * spread(w2[tok:], base, block)
        scaled = jnp.concatenate([mine, theirs], axis=0).astype(BF16)
        state = dot(pbt[base // gw], scaled)
        for q in range(PAIR):
            s_own[k + q] = state[:, q * WIDTH : (q + 1) * WIDTH]

    right = {"req": jnp.minimum(i + 1, R - 1)}
    left = {"req": jnp.maximum(i - 1, 0)}

    def l_copy(src, dst, up, k):
        return remote(src, dst, l_send.at[up], l_recv.at[k], right)

    def r_copy(src, dst, up, k):
        return remote(src, dst, r_send.at[up], r_recv.at[k], left)

    def state_l(k):
        return l_copy(s_lout.at[k], s_lin.at[k], 0, k)

    def own_l(k):
        return l_copy(s_own.at[k], s_lin.at[k], 0, k)

    def state_r(k):
        return r_copy(s_rout.at[k], s_rin.at[k], 0, k)

    def own_r(k):
        return r_copy(s_own.at[k], s_rin.at[k], 0, k)

    def carry_l():
        return l_copy(c_lout, c_lin, 1, K)

    def own_carry_l():
        return l_copy(c_own, c_lin, 1, K)

    def carry_r():
        return r_copy(c_rout, c_rin, 1, K)

    def own_carry_r():
        return r_copy(c_own, c_rin, 1, K)

    def carry_a():
        return remote(c_tot, c_ag, a_send.at[1], a_recv.at[RING], sib)

    def state_a(k):
        return remote(
            s_tot.at[k], s_ag.at[k], a_send.at[0], a_recv.at[k // PAIR % RING], sib
        )

    def pair_a(k):
        both = pl.ds(k, PAIR)
        return remote(
            s_tot.at[both], s_ag.at[both], a_send.at[0], a_recv.at[k // PAIR % RING], sib
        )

    def z_copy(j):
        rows = pl.ds(j, QUAD)
        return remote(st0.at[rows], st0.at[rows], z_send.at[0], z_recv.at[j // OCT], sib)

    def oct_z(j):
        rows = pl.ds(j, OCT)
        return remote(st0.at[rows], st0.at[rows], z_send.at[0], z_recv.at[j // OCT], sib)

    def push(source, sink, own, came, out_ref, relay, straight):
        @pl.when(source)
        def _():
            straight().start()

        @pl.when(jnp.logical_not(source))
        def _():
            relay().wait_recv()

            @pl.when(jnp.logical_not(sink))
            def _():
                out_ref[...] = own[...] + came[...]
                relay().start()

    def close(own, lin, lout, rin, tot, copy):
        @pl.when(first)
        def _():
            tot[...] = own[...] + rin[...]

        @pl.when(last)
        def _():
            tot[...] = own[...] + lin[...]

        @pl.when(jnp.logical_not(first | last))
        def _():
            tot[...] = lout[...] + rin[...]

        copy().start()

    def cont_chunk(owner, k):
        base = place(owner, k)
        j = owner * K + k
        at = pl.ds(base, wide_block)
        steered = (cxv[:, at].astype(F32) + mv[:, at]).astype(BF16)
        wide = steered.astype(F32)
        out[:, at] = skc[0:1, at] * wide
        scaled = (wide * spread(colw[...], base, wide_block)).astype(BF16)
        for q in range(QUAD):
            sc[j + q] = scaled[:, q * WIDTH : (q + 1) * WIDTH]

        @pl.when(s == 0)
        def _():
            state = dot(cbt[base // gw], scaled)
            for q in range(QUAD):
                st0[j + q] = state[:, q * WIDTH : (q + 1) * WIDTH]
            z_copy(j).start()

    def finish(owner, k, ready):
        base = place(owner, k)
        j = owner * K + k
        at = pl.ds(base, block)
        coming = jnp.concatenate([ready[k + q] for q in range(PAIR)], axis=1)
        before = jnp.concatenate([st0[j + q] for q in range(PAIR)], axis=1)
        start = coming + spread(carw[...], base, block) * mv[:, at]
        incoming = ((start + second * before) * fc[0:1, at]).astype(BF16)
        scaled = jnp.concatenate([sc[j + q] for q in range(PAIR)], axis=1)
        z = dot(gc[base // gw], jnp.concatenate([scaled, incoming], axis=0))
        mixed = out[:, at] + spread(roww[...], base, block) * z
        out[:, at] = mixed * gav[:, at]
        square = mixed * mixed
        folded = square[:, :LANES]
        for q in range(1, block // LANES):
            folded = folded + square[:, q * LANES : (q + 1) * LANES]
        return folded

    def within(k):
        return (k >= 0) & (k < K)

    second = jnp.where(s == 1, 1.0, 0.0).astype(F32)
    produce(jnp.int32(0))

    @pl.when(first)
    def _():
        own_l(0).start()

    @pl.when(last)
    def _():
        own_r(0).start()

    lane_group = lax.broadcasted_iota(jnp.int32, (nh, H), 1)
    carry = jnp.zeros((nh, H), F32)
    weight = thirds(w2[:, :H])
    rows = pl.ds(pl.multiple_of(s * nh, nh), nh)
    for g in range(Gd):
        inside = (lane_group >= g * per_group) & (lane_group < (g + 1) * per_group)
        part = dot(jnp.concatenate([pbt[g, rows]] * 3, axis=1), weight)
        carry = jnp.where(inside, part, carry)
    c_own[...] = carry

    for k in range(PAIR, AHEAD, PAIR):
        produce(jnp.int32(k))
    cdt_in.wait()
    ccum = running_sum(-rav[...] * cdv[...])
    ctot[...] = jnp.broadcast_to(ccum[T - 1 :, :], (8, H))

    @pl.when(s == 0)
    def _():
        d_copy().start()

    colw[:, :H] = jnp.exp(-ccum) * cdv[...]
    roww[:, :H] = jnp.exp(ccum)
    ssacc[...] = jnp.zeros_like(ssacc)
    for copy in later:
        copy.wait()
    entry = lax.broadcasted_iota(jnp.int32, tav.shape, 1) == mult_at[0]
    multiplier = jnp.sum(jnp.where(entry, tav[...], 0.0), axis=1, keepdims=True)
    wanted = lax.broadcasted_iota(jnp.int32, vecs.shape, 0) == behav_at[0]
    mv[...] = multiplier * jnp.sum(jnp.where(wanted, vev[...], 0.0), axis=0, keepdims=True)
    cbc_in.wait()
    lower = lax.broadcasted_iota(jnp.int32, (T, T), 0) >= lax.broadcasted_iota(
        jnp.int32, (T, T), 1
    )
    for g in range(Gd):
        bmat = cbv[:, 0, g, :].astype(F32)
        cmat = cbv[:, 1, g, :].astype(F32).astype(BF16)
        cbt[g] = bmat.T.astype(BF16)
        gmat = jnp.where(lower, dot_t(cmat, bmat.astype(BF16)), 0.0)
        gc[g] = jnp.concatenate([gmat.astype(BF16), cmat], axis=1)

    def row_of(value, to):
        value = padded(jnp.broadcast_to(value, (8, H)))
        lane = lax.broadcasted_iota(jnp.int32, (8, LANES), 1)
        for q in range(C // LANES):
            at = lax.shift_right_logical(lane, head.bit_length() - 1) + q * (LANES // head)
            to[:, q * LANES : (q + 1) * LANES] = jnp.take_along_axis(
                value, at, axis=1, mode="promise_in_bounds"
            )

    row_of(skv[...], skc)

    @pl.when(s == 0)
    def _():
        fc[...] = jnp.ones_like(fc)

    @pl.when(s == 1)
    def _():
        d_copy().wait_recv()
        row_of(jnp.exp(ctot_in[0:1, :]), fc)

    cx_in.wait()

    def step(m, unused):
        kl = m - SKEW_L * i
        kr = m - SKEW_R * hr
        kt = m - far
        kf = kt - LAG

        @pl.when(within(kr) & (kr + hr > 0))
        def _():
            push(
                last,
                first,
                s_own.at[kr],
                s_rin.at[kr],
                s_rout.at[kr],
                functools.partial(state_r, kr),
                functools.partial(own_r, kr),
            )

        @pl.when(within(kl) & (kl + i > 0))
        def _():
            push(
                first,
                last,
                s_own.at[kl],
                s_lin.at[kl],
                s_lout.at[kl],
                functools.partial(state_l, kl),
                functools.partial(own_l, kl),
            )

        @pl.when(kr == 0)
        def _():
            push(last, first, c_own, c_rin, c_rout, carry_r, own_carry_r)

        @pl.when(kl == 0)
        def _():
            push(first, last, c_own, c_lin, c_lout, carry_l, own_carry_l)

        @pl.when(within(kt))
        def _():
            close(
                s_own.at[kt],
                s_lin.at[kt],
                s_lout.at[kt],
                s_rin.at[kt],
                s_tot.at[kt],
                functools.partial(state_a, kt),
            )

        @pl.when(kt == 0)
        def _():
            close(c_own, c_lin, c_lout, c_rin, c_tot, carry_a)

        @pl.when((m % PAIR == 0) & (m + AHEAD < K))
        def _():
            produce(m + AHEAD)

        @pl.when(m < 2 * K // QUAD)
        def _():
            cont_chunk(jnp.where(m % 2 == 0, s, 1 - s), m // 2 * QUAD)

        @pl.when(kf == 0)
        def _():
            carry_a().wait_recv()
            carw[pl.ds(pl.multiple_of(s * nh, nh), nh), :H] = c_tot[...]
            carw[pl.ds(pl.multiple_of((1 - s) * nh, nh), nh), :H] = c_ag[...]

        @pl.when(within(kf) & (kf % PAIR == PAIR - 1))
        def _():
            k = kf - PAIR + 1
            pair_a(k).wait_recv()

            @pl.when((s == 1) & (k % OCT == 0))
            def _():
                oct_z(k).wait_recv()
                oct_z(k + K).wait_recv()

            ssacc[...] += finish(s, k, s_tot) + finish(1 - s, k, s_ag)

        return unused

    steps = K + max(SKEW_L, SKEW_R) * (R - 1) + LAG
    lax.fori_loop(0, steps, step, 0)

    folded = ssacc[...].T
    partial = folded[0:8]
    for q in range(1, LANES // 8):
        partial = partial + folded[q * 8 : (q + 1) * 8]
    ssl[x] = partial

    def p_copy(j, at):
        return remote(ssl.at[at], ssl.at[at], p_send.at[j], p_recv.at[at], {"tp": j})

    each(TP, x, lambda j: p_copy(j, x).start())

    x_copy(pxs, pxr, 0, 0).wait_send()
    remote(s_tot, s_ag, a_send.at[0], a_recv.at[0], sib).wait_send()
    u_x().wait_send()
    pb_x().wait_send()
    carry_a().wait_send()

    @pl.when(jnp.logical_not(last))
    def _():
        carry_l().wait_send()
        l_copy(s_lout, s_lin, 0, 0).wait_send()

    @pl.when(jnp.logical_not(first))
    def _():
        carry_r().wait_send()
        r_copy(s_rout, s_rin, 0, 0).wait_send()

    @pl.when(s == 0)
    def _():
        d_copy().wait_send()
        remote(st0, st0, z_send.at[0], z_recv.at[0], sib).wait_send()

    def told(j, carry):
        tot_copy(j, me).wait_send()
        return carry

    lax.fori_loop(0, me, told, 0)


    each(TP, x, lambda j: p_copy(j, j).wait_recv())
    meansq = jnp.sum(jnp.sum(ssl[...], axis=0), axis=0, keepdims=True) / (C * TP)
    scale_out[...] = jnp.broadcast_to(lax.rsqrt(meansq + 1e-05), scale_out.shape)
    each(TP, x, lambda j: p_copy(j, x).wait_send())


def local(
    prompt_x,
    prompt_b,
    prompt_dt,
    cont_x,
    cont_bc,
    cont_dt,
    decay_rate,
    skip_gain,
    norm_gain,
    steer_vecs,
    mult_table,
    mult_idx,
    behav_idx,
):
    R, TP = lax.axis_size("req"), lax.axis_size("tp")
    H = decay_rate.shape[0]
    tok, C = prompt_x.shape
    Gd, N = prompt_b.shape[1:]
    T = cont_x.shape[1]
    K = C // 2 // WIDTH
    NX = C // 2 // PIECE
    HP = max(H, LANES)
    def outside_of(*values):
        return tuple(pltpu.with_memory_space_constraint(v, pltpu.HBM) for v in values)

    args = outside_of(
        prompt_x,
        prompt_b,
        prompt_dt,
        cont_x[0],
        cont_bc[0],
        cont_dt[0],
        decay_rate[None],
        skip_gain[None],
        norm_gain[None],
        steer_vecs,
        mult_table[None],
    ) + (mult_idx, behav_idx)
    vmem, dma = pltpu.VMEM, pltpu.SemaphoreType.DMA
    inside = pl.BlockSpec(memory_space=pltpu.VMEM)
    outside = pl.BlockSpec(memory_space=pl.ANY)
    scalars = pl.BlockSpec(memory_space=pltpu.SMEM)
    part = (K, N, WIDTH)
    carried = (N // 2, H)
    scratch = (
        [
            vmem((tok, H), F32),
            vmem((tok, Gd, N), BF16),
            vmem((1, H), F32),
            vmem((1, H), F32),
            vmem((1, C), F32),
            vmem((1, mult_table.shape[0]), F32),
            vmem((tok, C), BF16),
            vmem((T, C), BF16),
            vmem(cont_bc.shape[1:], BF16),
            vmem((T, H), F32),
            vmem(steer_vecs.shape, F32),
        ]
        + [vmem((NX, tok, PIECE), F32)] * 2
        + [vmem((tok, H), F32)] * 2
        + [vmem((Gd, tok, N), F32)] * 2
        + [vmem((Gd, N, 2 * tok), BF16)]
        + [vmem((2 * tok, HP), F32)]
        + [vmem((T, HP), F32)] * 2
        + [vmem((Gd, T, T + N), BF16), vmem((Gd, N, T), BF16)]
        + [vmem((1, C), F32), vmem((8, C), F32), vmem((8, C), F32)]
        + [vmem((2 * R, 8, H), F32)]
        + [vmem((8, H), F32)] * 2
        + [vmem((2 * K, T, WIDTH), BF16)]
        + [vmem((2 * K, N, WIDTH), F32)]
        + [vmem(part, F32)] * 7
        + [vmem(carried, F32)] * 7
        + [vmem((N, HP), F32), vmem((T, LANES), F32), vmem((TP, 8, T), F32)]
        + [dma((NX + 11,))]
        + [dma((2 * R,))] * 2
        + [dma((3,)), dma((NX + 2,))]
        + [dma((2,)), dma((K + 1,))] * 2
        + [dma((2,)), dma((RING + 1,))]
        + [dma((1,)), dma((2 * K // OCT,))]
        + [dma((1,))] * 2
        + [dma((TP,))] * 2
    )
    mixed, scale = pl.pallas_call(
        functools.partial(kernel, R, TP, K, HP),
        out_shape=[jax.ShapeDtypeStruct((T, C), F32), jax.ShapeDtypeStruct((8, T), F32)],
        in_specs=[outside] * 11 + [scalars] * 2,
        out_specs=[inside, inside],
        scratch_shapes=scratch,
        compiler_params=pltpu.CompilerParams(
            collective_id=0, has_side_effects=True, vmem_limit_bytes=40 * 1024 * 1024
        ),
        name="sweep",
    )(*args)
    return (mixed * scale[0][:, None]).astype(BF16)[None]


def solution(mesh):
    return jax.shard_map(
        local,
        mesh=mesh,
        in_specs=(
            P(("parts", "req", "sp"), "tp"),
            P(("parts", "req", "sp"), "tp", None),
            P(("parts", "req", "sp"), "tp"),
            P(("parts", "req"), "sp", "tp"),
            P(("parts", "req"), "sp", None, "tp", None),
            P(("parts", "req"), "sp", "tp"),
            P("tp"),
            P("tp"),
            P("tp"),
            P(None, "tp"),
            P(),
            P(("parts", "req")),
            P(("parts", "req")),
        ),
        out_specs=P(("parts", "req"), "sp", "tp"),
        check_vma=False,
    )
```

```python
import functools

import jax
import jax.numpy as jnp
from jax import lax
from jax.experimental import pallas as pl
from jax.experimental.pallas import tpu as pltpu
from jax.sharding import PartitionSpec as P

MESH = pl.DeviceIdType.MESH
F32 = jnp.float32
BF16 = jnp.bfloat16
LANES = 128
WIDTH = 128
SPLIT = 1
PAIR = 2
QUAD = 4
OCT = 8
PIECE = 1024
RING = 8
TURN = 4
SETUP = 4
AHEAD = 4
SKEW_L = 3
SKEW_R = 2


def dot(a, b):
    return jnp.dot(a, b, preferred_element_type=F32)


def dot_t(a, b):
    return lax.dot_general(a, b, (((1,), (1,)), ((), ())), preferred_element_type=F32)


def thirds(value):
    lead = value.astype(BF16)
    rest = value - lead.astype(F32)
    mid = rest.astype(BF16)
    low = (rest - mid.astype(F32)).astype(BF16)
    return jnp.concatenate([lead, mid, low], axis=0)


def running_sum(rows):
    length = rows.shape[0]
    lower = lax.broadcasted_iota(jnp.int32, (length, length), 0) >= lax.broadcasted_iota(
        jnp.int32, (length, length), 1
    )
    ones = jnp.where(lower, 1.0, 0.0).astype(BF16)
    return dot(jnp.concatenate([ones] * 3, axis=1), thirds(rows))


def kernel(
    R,
    TP,
    K,
    HP,
    DEEP,
    px,
    pb,
    pdt,
    cx,
    cbc,
    cdt,
    rate,
    skip,
    gain,
    vecs,
    table,
    mult_at,
    behav_at,
    out,
    scale_out,
    pdv,
    pbv,
    rav,
    skv,
    gav,
    tav,
    pxv,
    cxv,
    cbv,
    cdv,
    vev,
    pxs,
    pxr,
    us,
    ur,
    pbs,
    pbr,
    pbt,
    w2,
    colw,
    roww,
    gc,
    cbt,
    mv,
    skc,
    fc,
    tots,
    ctot,
    ctot_in,
    sc,
    st0,
    s_own,
    s_lin,
    s_lout,
    s_rin,
    s_rout,
    s_tot,
    s_ag,
    c_own,
    c_lin,
    c_lout,
    c_rin,
    c_rout,
    c_tot,
    c_ag,
    carw,
    ssacc,
    ssl,
    h_sem,
    t_send,
    t_recv,
    x_send,
    x_recv,
    l_send,
    l_recv,
    r_send,
    r_recv,
    a_send,
    a_recv,
    z_send,
    z_recv,
    d_send,
    d_recv,
    p_send,
    p_recv,
):
    i = lax.axis_index("req")
    s = lax.axis_index("sp")
    x = lax.axis_index("tp")
    me = i * 2 + s
    other = i * 2 + 1 - s
    hr = R - 1 - i
    far = jnp.maximum(SKEW_L * i, SKEW_R * hr)
    tok, H = pdt.shape
    block = WIDTH * PAIR
    wide_block = WIDTH * QUAD

    C = px.shape[1]
    Gd, N = pb.shape[1:]
    T = cx.shape[0]
    U = K * SPLIT
    ROWS = N // SPLIT
    RUN = PAIR * SPLIT
    BEFORE = AHEAD * SPLIT
    half = C // 2
    head = C // H
    gw = C // Gd
    per_group = H // Gd
    nh = N // 2
    NX = half // PIECE
    PER = PIECE // WIDTH
    sib = {"sp": 1 - s}
    first, last = i == 0, i == R - 1

    def each(count, skip_index, body):
        def turn(j, carry):
            @pl.when(j != skip_index)
            def _():
                body(j)

            return carry

        lax.fori_loop(0, count, turn, 0)

    def peer(j):
        return {"req": j // 2, "sp": j % 2}

    def remote(src, dst, send, recv, device):
        return pltpu.make_async_remote_copy(
            src_ref=src,
            dst_ref=dst,
            send_sem=send,
            recv_sem=recv,
            device_id=device,
            device_id_type=MESH,
        )

    def h_copy(src, dst, k):
        return pltpu.make_async_copy(src, dst, h_sem.at[k])

    def piece_at(owner, q):
        return pl.ds(pl.multiple_of(owner * half + q * PIECE, PIECE), PIECE)

    own_half = pl.ds(pl.multiple_of(s * half, half), half)
    pieces = [
        h_copy(px.at[:, piece_at(1 - s, q)], pxv.at[:, piece_at(1 - s, q)], q) for q in range(NX)
    ]
    early = [h_copy(pdt, pdv, NX), h_copy(rate, rav, NX + 1), h_copy(pb, pbv, NX + 2)]
    px_own = h_copy(px.at[:, own_half], pxv.at[:, own_half], NX + 3)
    cdt_in = h_copy(cdt, cdv, NX + 4)
    cbc_in = h_copy(cbc, cbv, NX + 5)
    later = [
        h_copy(vecs, vev, NX + 6),
        h_copy(table, tav, NX + 7),
        h_copy(skip, skv, NX + 8),
        h_copy(gain, gav, NX + 9),
    ]
    cx_in = h_copy(cx, cxv, NX + 10)
    barrier = pltpu.get_barrier_semaphore()

    def greet(j, carry):
        @pl.when((j > me) | (j == other) | (j == me - 2))
        def _():
            pl.semaphore_signal(barrier, inc=1, device_id=peer(j), device_id_type=MESH)

        return carry

    lax.fori_loop(0, 2 * R, greet, 0)
    each(
        TP,
        x,
        lambda j: pl.semaphore_signal(barrier, inc=1, device_id={"tp": j}, device_id_type=MESH),
    )
    for copy in pieces[:1] + early + pieces[1:]:
        copy.start()
    for copy in [px_own, cdt_in, cbc_in] + later + [cx_in]:
        copy.start()

    pieces[0].wait()
    pxs[0] = pxv[:, piece_at(1 - s, 0)].astype(F32)
    early[2].wait()
    for g in range(Gd):
        pbs[g] = pbv[:, g, :].astype(F32)
    greeted = me + (1 - s) + jnp.where(i < R - 1, 1, 0) + TP - 1
    pl.semaphore_wait(barrier, greeted)

    def tot_copy(j, slot):
        return remote(tots.at[slot], tots.at[slot], t_send.at[j], t_recv.at[slot], peer(j))

    def x_copy(src, dst, up, k):
        return remote(src, dst, x_send.at[up], x_recv.at[k], sib)

    def px_x(q):
        return x_copy(pxs.at[q], pxr.at[q], 0, q)

    def u_x():
        return x_copy(us, ur, 1, NX)

    def pb_x():
        return x_copy(pbs, pbr, 2, NX + 1)

    def d_copy():
        return remote(ctot, ctot_in, d_send.at[0], d_recv.at[0], sib)

    px_x(0).start()
    pb_x().start()
    early[0].wait()
    early[1].wait()
    cum = running_sum(-rav[...] * pdv[...])
    total = cum[tok - 1 :, :]
    tots[me] = jnp.broadcast_to(total, (8, H))
    us[...] = jnp.exp(total - cum) * pdv[...]
    u_x().start()

    def tell(j, carry):
        tot_copy(j, me).start()
        return carry

    lax.fori_loop(0, me, tell, 0)

    for q in range(1, NX):
        pieces[q].wait()
        pxs[q] = pxv[:, piece_at(1 - s, q)].astype(F32)
        px_x(q).start()

    def padded(value):
        return jnp.concatenate([value] * (HP // H), axis=1) if HP > H else value

    def spread(value, base, width):
        lane = lax.broadcasted_iota(jnp.int32, (value.shape[0], LANES), 1)
        shift = head.bit_length() - 1
        parts = []
        for q in range(width // LANES):
            at = lax.shift_right_logical(lane, shift) + (base // head + q * (LANES // head))
            parts.append(jnp.take_along_axis(value, at, axis=1, mode="promise_in_bounds"))
        return parts[0] if len(parts) == 1 else jnp.concatenate(parts, axis=1)

    def place(owner, k):
        return pl.multiple_of(owner * half + k * WIDTH, WIDTH)

    u_x().wait_recv()
    pb_x().wait_recv()
    for g in range(Gd):
        pbt[g] = jnp.concatenate([pbs[g], pbr[g]], axis=0).T.astype(BF16)
    px_own.wait()

    def heard(j, carry):
        tot_copy(j, j).wait_recv()
        return carry

    lax.fori_loop(me + 1, 2 * R, heard, 0)

    slot = lax.broadcasted_iota(jnp.int32, tots.shape, 0)
    every = tots[...]
    after_me = jnp.sum(jnp.where(slot > me, every, 0.0), axis=0)[0:1, :]
    after_other = jnp.sum(jnp.where(slot > other, every, 0.0), axis=0)[0:1, :]
    w2[:tok, :H] = us[...] * jnp.exp(after_me)
    w2[tok:, :H] = ur[...] * jnp.exp(after_other)

    def produce(k):
        base = place(s, k)

        @pl.when(k % PER == 0)
        def _():
            px_x(k // PER).wait_recv()

        at = pl.ds(pl.multiple_of((k % PER) * WIDTH, WIDTH), block)
        mine = pxv[:, pl.ds(base, block)].astype(F32) * spread(w2[:tok], base, block)
        theirs = pxr[k // PER, :, at] * spread(w2[tok:], base, block)
        scaled = jnp.concatenate([mine, theirs], axis=0).astype(BF16)
        state = dot(pbt[base // gw], scaled)
        for q in range(PAIR):
            for v in range(SPLIT):
                s_own[(k + q) * SPLIT + v] = state[
                    v * ROWS : (v + 1) * ROWS, q * WIDTH : (q + 1) * WIDTH
                ]

    right = {"req": jnp.minimum(i + 1, R - 1)}
    left = {"req": jnp.maximum(i - 1, 0)}

    def l_copy(src, dst, up, k):
        return remote(src, dst, l_send.at[up], l_recv.at[k], right)

    def r_copy(src, dst, up, k):
        return remote(src, dst, r_send.at[up], r_recv.at[k], left)

    def state_l(k):
        return l_copy(s_lout.at[k], s_lin.at[k], 0, k % DEEP)

    def own_l(k):
        return l_copy(s_own.at[k], s_lin.at[k], 0, k % DEEP)

    def state_r(k):
        return r_copy(s_rout.at[k], s_rin.at[k], 0, k % DEEP)

    def own_r(k):
        return r_copy(s_own.at[k], s_rin.at[k], 0, k % DEEP)

    def carry_l():
        return l_copy(c_lout, c_lin, 1, DEEP)

    def own_carry_l():
        return l_copy(c_own, c_lin, 1, DEEP)

    def carry_r():
        return r_copy(c_rout, c_rin, 1, DEEP)

    def own_carry_r():
        return r_copy(c_own, c_rin, 1, DEEP)

    def carry_a():
        return remote(c_tot, c_ag, a_send.at[1], a_recv.at[RING], sib)

    def state_a(k):
        rows = pl.ds(k * SPLIT, SPLIT)
        return remote(
            s_tot.at[rows], s_ag.at[rows], a_send.at[0], a_recv.at[k // PAIR % RING], sib
        )

    def pair_a(k):
        rows = pl.ds(k * SPLIT, RUN)
        return remote(
            s_tot.at[rows], s_ag.at[rows], a_send.at[0], a_recv.at[k // PAIR % RING], sib
        )

    def z_copy(j):
        rows = pl.ds(j, QUAD)
        return remote(st0.at[rows], st0.at[rows], z_send.at[0], z_recv.at[j // OCT], sib)

    def oct_z(j):
        rows = pl.ds(j, OCT)
        return remote(st0.at[rows], st0.at[rows], z_send.at[0], z_recv.at[j // OCT], sib)

    def push(source, sink, own, came, out_ref, relay, straight):
        @pl.when(source)
        def _():
            straight().start()

        @pl.when(jnp.logical_not(source))
        def _():
            relay().wait_recv()

            @pl.when(jnp.logical_not(sink))
            def _():
                out_ref[...] = own[...] + came[...]
                relay().start()

    def close(own, lin, lout, rin, tot):
        @pl.when(first)
        def _():
            tot[...] = own[...] + rin[...]

        @pl.when(last)
        def _():
            tot[...] = own[...] + lin[...]

        @pl.when(jnp.logical_not(first | last))
        def _():
            tot[...] = lout[...] + rin[...]

    def cont_chunk(owner, k):
        base = place(owner, k)
        j = owner * K + k
        at = pl.ds(base, wide_block)
        steered = (cxv[:, at].astype(F32) + mv[:, at]).astype(BF16)
        wide = steered.astype(F32)
        out[:, at] = skc[0:1, at] * wide
        scaled = (wide * spread(colw[...], base, wide_block)).astype(BF16)
        for q in range(QUAD):
            sc[j + q] = scaled[:, q * WIDTH : (q + 1) * WIDTH]

        @pl.when(s == 0)
        def _():
            state = dot(cbt[base // gw], scaled)
            for q in range(QUAD):
                st0[j + q] = state[:, q * WIDTH : (q + 1) * WIDTH]
            z_copy(j).start()

    def finish(owner, k, ready):
        base = place(owner, k)
        j = owner * K + k
        at = pl.ds(base, block)
        coming = jnp.concatenate(
            [
                jnp.concatenate([ready[(k + q) * SPLIT + v] for v in range(SPLIT)], axis=0)
                for q in range(PAIR)
            ],
            axis=1,
        )
        before = jnp.concatenate([st0[j + q] for q in range(PAIR)], axis=1)
        start = coming + spread(carw[...], base, block) * mv[:, at]
        incoming = ((start + second * before) * fc[0:1, at]).astype(BF16)
        scaled = jnp.concatenate([sc[j + q] for q in range(PAIR)], axis=1)
        z = dot(gc[base // gw], jnp.concatenate([scaled, incoming], axis=0))
        mixed = out[:, at] + spread(roww[...], base, block) * z
        out[:, at] = mixed * gav[:, at]
        square = mixed * mixed
        folded = square[:, :LANES]
        for q in range(1, block // LANES):
            folded = folded + square[:, q * LANES : (q + 1) * LANES]
        return folded

    def within(k):
        return (k >= 0) & (k < U)

    second = jnp.where(s == 1, 1.0, 0.0).astype(F32)
    for k in range(0, AHEAD, PAIR):
        produce(jnp.int32(k))

        @pl.when(first)
        def _():
            for q in range(RUN):
                own_l(jnp.int32(k * SPLIT + q)).start()

        @pl.when(last)
        def _():
            for q in range(RUN):
                own_r(jnp.int32(k * SPLIT + q)).start()

    def sum_carry():
        lane_group = lax.broadcasted_iota(jnp.int32, (nh, H), 1)
        carry = jnp.zeros((nh, H), F32)
        weight = thirds(w2[:, :H])
        rows = pl.ds(pl.multiple_of(s * nh, nh), nh)
        for g in range(Gd):
            inside = (lane_group >= g * per_group) & (lane_group < (g + 1) * per_group)
            part = dot(jnp.concatenate([pbt[g, rows]] * 3, axis=1), weight)
            carry = jnp.where(inside, part, carry)
        c_own[...] = carry

    def cont_decays():
        cdt_in.wait()
        ccum = running_sum(-rav[...] * cdv[...])
        ctot[...] = jnp.broadcast_to(ccum[T - 1 :, :], (8, H))

        @pl.when(s == 0)
        def _():
            d_copy().start()

        colw[:, :H] = jnp.exp(-ccum) * cdv[...]
        roww[:, :H] = jnp.exp(ccum)
        ssacc[...] = jnp.zeros_like(ssacc)

    def row_of(value, to):
        value = padded(jnp.broadcast_to(value, (8, H)))
        lane = lax.broadcasted_iota(jnp.int32, (8, LANES), 1)
        for q in range(C // LANES):
            at = lax.shift_right_logical(lane, head.bit_length() - 1) + q * (LANES // head)
            to[:, q * LANES : (q + 1) * LANES] = jnp.take_along_axis(
                value, at, axis=1, mode="promise_in_bounds"
            )

    def channel_rows():
        for copy in later:
            copy.wait()
        entry = lax.broadcasted_iota(jnp.int32, tav.shape, 1) == mult_at[0]
        multiplier = jnp.sum(jnp.where(entry, tav[...], 0.0), axis=1, keepdims=True)
        wanted = lax.broadcasted_iota(jnp.int32, vecs.shape, 0) == behav_at[0]
        mv[...] = multiplier * jnp.sum(jnp.where(wanted, vev[...], 0.0), axis=0, keepdims=True)
        row_of(skv[...], skc)

        @pl.when(s == 0)
        def _():
            fc[...] = jnp.ones_like(fc)

        @pl.when(s == 1)
        def _():
            d_copy().wait_recv()
            row_of(jnp.exp(ctot_in[0:1, :]), fc)

    def group_products():
        cbc_in.wait()
        lower = lax.broadcasted_iota(jnp.int32, (T, T), 0) >= lax.broadcasted_iota(
            jnp.int32, (T, T), 1
        )
        for g in range(Gd):
            bmat = cbv[:, 0, g, :].astype(F32)
            cmat = cbv[:, 1, g, :].astype(F32).astype(BF16)
            cbt[g] = bmat.T.astype(BF16)
            gmat = jnp.where(lower, dot_t(cmat, bmat.astype(BF16)), 0.0)
            gc[g] = jnp.concatenate([gmat.astype(BF16), cmat], axis=1)
        cx_in.wait()

    def step(m, unused):
        kl = m - SKEW_L * i
        kr = m - SKEW_R * hr
        kt = m - far
        kf = kt - RUN // 2

        @pl.when(within(kr) & ((kr >= BEFORE) | (hr > 0)))
        def _():
            push(
                last,
                first,
                s_own.at[kr],
                s_rin.at[kr],
                s_rout.at[kr],
                functools.partial(state_r, kr),
                functools.partial(own_r, kr),
            )

        @pl.when(within(kl) & ((kl >= BEFORE) | (i > 0)))
        def _():
            push(
                first,
                last,
                s_own.at[kl],
                s_lin.at[kl],
                s_lout.at[kl],
                functools.partial(state_l, kl),
                functools.partial(own_l, kl),
            )

        @pl.when(kr == TURN)
        def _():
            push(last, first, c_own, c_rin, c_rout, carry_r, own_carry_r)

        @pl.when(kl == TURN)
        def _():
            push(first, last, c_own, c_lin, c_lout, carry_l, own_carry_l)

        @pl.when(within(kt))
        def _():
            close(s_own.at[kt], s_lin.at[kt], s_lout.at[kt], s_rin.at[kt], s_tot.at[kt])

        @pl.when(within(kt) & (kt % SPLIT == SPLIT - 1))
        def _():
            state_a(kt // SPLIT).start()

        @pl.when(kt == TURN)
        def _():
            close(c_own, c_lin, c_lout, c_rin, c_tot)
            carry_a().start()

        @pl.when((m % RUN == 0) & (m + BEFORE < U))
        def _():
            produce(m // SPLIT + AHEAD)

        for number, work in enumerate((sum_carry, cont_decays, channel_rows, group_products)):
            pl.when(m == number)(work)

        @pl.when((m >= SETUP) & (m < SETUP + 2 * K // QUAD))
        def _():
            turn = m - SETUP
            cont_chunk(jnp.where(turn % 2 == 0, s, 1 - s), turn // 2 * QUAD)

        @pl.when(kt == TURN + 1)
        def _():
            carry_a().wait_recv()

            @pl.when(s == 1)
            def _():
                oct_z(0).wait_recv()
                oct_z(K).wait_recv()

            carw[pl.ds(pl.multiple_of(s * nh, nh), nh), :H] = c_tot[...]
            carw[pl.ds(pl.multiple_of((1 - s) * nh, nh), nh), :H] = c_ag[...]

        @pl.when((kt > TURN) & (kt < U) & (kt % RUN == RUN - 1))
        def _():
            k = kt // SPLIT - PAIR + 1

            @pl.when((s == 1) & (k % OCT == 0))
            def _():
                oct_z(k).wait_recv()
                oct_z(k + K).wait_recv()

            ssacc[...] += finish(s, k, s_tot)

        @pl.when((kf > TURN) & (kf < U) & (kf % RUN == RUN - 1))
        def _():
            k = kf // SPLIT - PAIR + 1
            pair_a(k).wait_recv()
            ssacc[...] += finish(1 - s, k, s_ag)

        @pl.when((kt >= 2 * TURN) & (kt < 3 * TURN) & (kt % RUN == 0))
        def _():
            k = (kt - 2 * TURN) // SPLIT
            ssacc[...] += finish(s, k, s_tot)
            pair_a(k).wait_recv()
            ssacc[...] += finish(1 - s, k, s_ag)

        return unused

    steps = U + max(SKEW_L, SKEW_R) * (R - 1) + RUN // 2
    lax.fori_loop(0, steps, step, 0)

    folded = ssacc[...].T
    partial = folded[0:8]
    for q in range(1, LANES // 8):
        partial = partial + folded[q * 8 : (q + 1) * 8]
    ssl[x] = partial

    def p_copy(j, at):
        return remote(ssl.at[at], ssl.at[at], p_send.at[j], p_recv.at[at], {"tp": j})

    each(TP, x, lambda j: p_copy(j, x).start())

    x_copy(pxs, pxr, 0, 0).wait_send()
    remote(s_tot, s_ag, a_send.at[0], a_recv.at[0], sib).wait_send()
    u_x().wait_send()
    pb_x().wait_send()
    carry_a().wait_send()

    @pl.when(jnp.logical_not(last))
    def _():
        carry_l().wait_send()
        l_copy(s_lout, s_lin, 0, 0).wait_send()

    @pl.when(jnp.logical_not(first))
    def _():
        carry_r().wait_send()
        r_copy(s_rout, s_rin, 0, 0).wait_send()

    @pl.when(s == 0)
    def _():
        d_copy().wait_send()
        remote(st0, st0, z_send.at[0], z_recv.at[0], sib).wait_send()

    def told(j, carry):
        tot_copy(j, me).wait_send()
        return carry

    lax.fori_loop(0, me, told, 0)


    each(TP, x, lambda j: p_copy(j, j).wait_recv())
    meansq = jnp.sum(jnp.sum(ssl[...], axis=0), axis=0, keepdims=True) / (C * TP)
    scale_out[...] = jnp.broadcast_to(lax.rsqrt(meansq + 1e-05), scale_out.shape)
    each(TP, x, lambda j: p_copy(j, x).wait_send())


def local(
    prompt_x,
    prompt_b,
    prompt_dt,
    cont_x,
    cont_bc,
    cont_dt,
    decay_rate,
    skip_gain,
    norm_gain,
    steer_vecs,
    mult_table,
    mult_idx,
    behav_idx,
):
    R, TP = lax.axis_size("req"), lax.axis_size("tp")
    H = decay_rate.shape[0]
    tok, C = prompt_x.shape
    Gd, N = prompt_b.shape[1:]
    T = cont_x.shape[1]
    K = C // 2 // WIDTH
    NX = C // 2 // PIECE
    HP = max(H, LANES)
    DEEP = min(K * SPLIT, (R - 1) * max(SKEW_L, SKEW_R) + SKEW_L + SKEW_R)
    def outside_of(*values):
        return tuple(pltpu.with_memory_space_constraint(v, pltpu.HBM) for v in values)

    args = outside_of(
        prompt_x,
        prompt_b,
        prompt_dt,
        cont_x[0],
        cont_bc[0],
        cont_dt[0],
        decay_rate[None],
        skip_gain[None],
        norm_gain[None],
        steer_vecs,
        mult_table[None],
    ) + (mult_idx, behav_idx)
    vmem, dma = pltpu.VMEM, pltpu.SemaphoreType.DMA
    inside = pl.BlockSpec(memory_space=pltpu.VMEM)
    outside = pl.BlockSpec(memory_space=pl.ANY)
    scalars = pl.BlockSpec(memory_space=pltpu.SMEM)
    part = (K * SPLIT, N // SPLIT, WIDTH)
    carried = (N // 2, H)
    scratch = (
        [
            vmem((tok, H), F32),
            vmem((tok, Gd, N), BF16),
            vmem((1, H), F32),
            vmem((1, H), F32),
            vmem((1, C), F32),
            vmem((1, mult_table.shape[0]), F32),
            vmem((tok, C), BF16),
            vmem((T, C), BF16),
            vmem(cont_bc.shape[1:], BF16),
            vmem((T, H), F32),
            vmem(steer_vecs.shape, F32),
        ]
        + [vmem((NX, tok, PIECE), F32)] * 2
        + [vmem((tok, H), F32)] * 2
        + [vmem((Gd, tok, N), F32)] * 2
        + [vmem((Gd, N, 2 * tok), BF16)]
        + [vmem((2 * tok, HP), F32)]
        + [vmem((T, HP), F32)] * 2
        + [vmem((Gd, T, T + N), BF16), vmem((Gd, N, T), BF16)]
        + [vmem((1, C), F32), vmem((8, C), F32), vmem((8, C), F32)]
        + [vmem((2 * R, 8, H), F32)]
        + [vmem((8, H), F32)] * 2
        + [vmem((2 * K, T, WIDTH), BF16)]
        + [vmem((2 * K, N, WIDTH), F32)]
        + [vmem(part, F32)] * 7
        + [vmem(carried, F32)] * 7
        + [vmem((N, HP), F32), vmem((T, LANES), F32), vmem((TP, 8, T), F32)]
        + [dma((NX + 11,))]
        + [dma((2 * R,))] * 2
        + [dma((3,)), dma((NX + 2,))]
        + [dma((2,)), dma((DEEP + 1,))] * 2
        + [dma((2,)), dma((RING + 1,))]
        + [dma((1,)), dma((2 * K // OCT,))]
        + [dma((1,))] * 2
        + [dma((TP,))] * 2
    )
    mixed, scale = pl.pallas_call(
        functools.partial(kernel, R, TP, K, HP, DEEP),
        out_shape=[jax.ShapeDtypeStruct((T, C), F32), jax.ShapeDtypeStruct((8, T), F32)],
        in_specs=[outside] * 11 + [scalars] * 2,
        out_specs=[inside, inside],
        scratch_shapes=scratch,
        compiler_params=pltpu.CompilerParams(
            collective_id=0, has_side_effects=True, vmem_limit_bytes=40 * 1024 * 1024
        ),
        name="sweep",
    )(*args)
    return (mixed * scale[0][:, None]).astype(BF16)[None]


def solution(mesh):
    return jax.shard_map(
        local,
        mesh=mesh,
        in_specs=(
            P(("parts", "req", "sp"), "tp"),
            P(("parts", "req", "sp"), "tp", None),
            P(("parts", "req", "sp"), "tp"),
            P(("parts", "req"), "sp", "tp"),
            P(("parts", "req"), "sp", None, "tp", None),
            P(("parts", "req"), "sp", "tp"),
            P("tp"),
            P("tp"),
            P("tp"),
            P(None, "tp"),
            P(),
            P(("parts", "req")),
            P(("parts", "req")),
        ),
        out_specs=P(("parts", "req"), "sp", "tp"),
        check_vma=False,
    )
```

```python
import functools

import jax
import jax.numpy as jnp
from jax import lax
from jax.experimental import pallas as pl
from jax.experimental.pallas import tpu as pltpu
from jax.sharding import PartitionSpec as P

MESH = pl.DeviceIdType.MESH
F32 = jnp.float32
BF16 = jnp.bfloat16
LANES = 128
WIDTH = 128
SPLIT = 1
PAIR = 2
QUAD = 4
OCT = 8
PIECE = 1024
RING = 8
TURN = 4 * SPLIT
SETUP = 4
AHEAD = 4
SKEW_L = 3
SKEW_R = 2


def dot(a, b):
    return jnp.dot(a, b, preferred_element_type=F32)


def dot_t(a, b):
    return lax.dot_general(a, b, (((1,), (1,)), ((), ())), preferred_element_type=F32)


def thirds(value):
    lead = value.astype(BF16)
    rest = value - lead.astype(F32)
    mid = rest.astype(BF16)
    low = (rest - mid.astype(F32)).astype(BF16)
    return jnp.concatenate([lead, mid, low], axis=0)


def running_sum(rows):
    length = rows.shape[0]
    lower = lax.broadcasted_iota(jnp.int32, (length, length), 0) >= lax.broadcasted_iota(
        jnp.int32, (length, length), 1
    )
    ones = jnp.where(lower, 1.0, 0.0).astype(BF16)
    return dot(jnp.concatenate([ones] * 3, axis=1), thirds(rows))


def kernel(
    R,
    TP,
    K,
    HP,
    DEEP,
    px,
    pb,
    pdt,
    cx,
    cbc,
    cdt,
    rate,
    skip,
    gain,
    vecs,
    table,
    mult_at,
    behav_at,
    out,
    scale_out,
    pdv,
    pbv,
    rav,
    skv,
    gav,
    tav,
    pxv,
    cxv,
    cbv,
    cdv,
    vev,
    pxs,
    pxr,
    us,
    ur,
    pbs,
    pbr,
    pbt,
    w2,
    colw,
    roww,
    gc,
    cbt,
    mv,
    skc,
    fc,
    tots,
    ctot,
    ctot_in,
    sc,
    st0,
    s_own,
    s_lin,
    s_lout,
    s_rin,
    s_rout,
    s_tot,
    s_ag,
    c_own,
    c_lin,
    c_lout,
    c_rin,
    c_rout,
    c_tot,
    c_ag,
    carw,
    ssacc,
    ssl,
    h_sem,
    t_send,
    t_recv,
    x_send,
    x_recv,
    l_send,
    l_recv,
    r_send,
    r_recv,
    a_send,
    a_recv,
    z_send,
    z_recv,
    d_send,
    d_recv,
    p_send,
    p_recv,
):
    i = lax.axis_index("req")
    s = lax.axis_index("sp")
    x = lax.axis_index("tp")
    me = i * 2 + s
    other = i * 2 + 1 - s
    hr = R - 1 - i
    far = jnp.maximum(SKEW_L * i, SKEW_R * hr)
    tok, H = pdt.shape
    block = WIDTH * PAIR
    wide_block = WIDTH * QUAD

    C = px.shape[1]
    Gd, N = pb.shape[1:]
    T = cx.shape[0]
    U = K * SPLIT
    ROWS = N // SPLIT
    RUN = PAIR * SPLIT
    BEFORE = AHEAD * SPLIT
    half = C // 2
    head = C // H
    gw = C // Gd
    per_group = H // Gd
    nh = N // 2
    NX = half // PIECE
    PER = PIECE // WIDTH
    sib = {"sp": 1 - s}
    first, last = i == 0, i == R - 1

    def each(count, skip_index, body):
        def turn(j, carry):
            @pl.when(j != skip_index)
            def _():
                body(j)

            return carry

        lax.fori_loop(0, count, turn, 0)

    def peer(j):
        return {"req": j // 2, "sp": j % 2}

    def remote(src, dst, send, recv, device):
        return pltpu.make_async_remote_copy(
            src_ref=src,
            dst_ref=dst,
            send_sem=send,
            recv_sem=recv,
            device_id=device,
            device_id_type=MESH,
        )

    def h_copy(src, dst, k):
        return pltpu.make_async_copy(src, dst, h_sem.at[k])

    def piece_at(owner, q):
        return pl.ds(pl.multiple_of(owner * half + q * PIECE, PIECE), PIECE)

    own_half = pl.ds(pl.multiple_of(s * half, half), half)
    pieces = [
        h_copy(px.at[:, piece_at(1 - s, q)], pxv.at[:, piece_at(1 - s, q)], q) for q in range(NX)
    ]
    early = [h_copy(pdt, pdv, NX), h_copy(rate, rav, NX + 1), h_copy(pb, pbv, NX + 2)]
    px_own = h_copy(px.at[:, own_half], pxv.at[:, own_half], NX + 3)
    cdt_in = h_copy(cdt, cdv, NX + 4)
    cbc_in = h_copy(cbc, cbv, NX + 5)
    later = [
        h_copy(vecs, vev, NX + 6),
        h_copy(table, tav, NX + 7),
        h_copy(skip, skv, NX + 8),
        h_copy(gain, gav, NX + 9),
    ]
    cx_in = h_copy(cx, cxv, NX + 10)
    barrier = pltpu.get_barrier_semaphore()

    def greet(j, carry):
        @pl.when((j > me) | (j == other) | (j == me - 2))
        def _():
            pl.semaphore_signal(barrier, inc=1, device_id=peer(j), device_id_type=MESH)

        return carry

    lax.fori_loop(0, 2 * R, greet, 0)
    each(
        TP,
        x,
        lambda j: pl.semaphore_signal(barrier, inc=1, device_id={"tp": j}, device_id_type=MESH),
    )
    for copy in pieces[:1] + early + pieces[1:]:
        copy.start()
    for copy in [px_own, cdt_in, cbc_in] + later + [cx_in]:
        copy.start()

    pieces[0].wait()
    pxs[0] = pxv[:, piece_at(1 - s, 0)].astype(F32)
    early[2].wait()
    for g in range(Gd):
        pbs[g] = pbv[:, g, :].astype(F32)
    greeted = me + (1 - s) + jnp.where(i < R - 1, 1, 0) + TP - 1
    pl.semaphore_wait(barrier, greeted)

    def tot_copy(j, slot):
        return remote(tots.at[slot], tots.at[slot], t_send.at[j], t_recv.at[slot], peer(j))

    def x_copy(src, dst, up, k):
        return remote(src, dst, x_send.at[up], x_recv.at[k], sib)

    def px_x(q):
        return x_copy(pxs.at[q], pxr.at[q], 0, q)

    def u_x():
        return x_copy(us, ur, 1, NX)

    def pb_x():
        return x_copy(pbs, pbr, 2, NX + 1)

    def d_copy():
        return remote(ctot, ctot_in, d_send.at[0], d_recv.at[0], sib)

    px_x(0).start()
    pb_x().start()
    early[0].wait()
    early[1].wait()
    cum = running_sum(-rav[...] * pdv[...])
    total = cum[tok - 1 :, :]
    tots[me] = jnp.broadcast_to(total, (8, H))
    us[...] = jnp.exp(total - cum) * pdv[...]
    u_x().start()

    def tell(j, carry):
        tot_copy(j, me).start()
        return carry

    lax.fori_loop(0, me, tell, 0)

    for q in range(1, NX):
        pieces[q].wait()
        pxs[q] = pxv[:, piece_at(1 - s, q)].astype(F32)
        px_x(q).start()

    def padded(value):
        return jnp.concatenate([value] * (HP // H), axis=1) if HP > H else value

    def spread(value, base, width):
        lane = lax.broadcasted_iota(jnp.int32, (value.shape[0], LANES), 1)
        shift = head.bit_length() - 1
        parts = []
        for q in range(width // LANES):
            at = lax.shift_right_logical(lane, shift) + (base // head + q * (LANES // head))
            parts.append(jnp.take_along_axis(value, at, axis=1, mode="promise_in_bounds"))
        return parts[0] if len(parts) == 1 else jnp.concatenate(parts, axis=1)

    def place(owner, k):
        return pl.multiple_of(owner * half + k * WIDTH, WIDTH)

    u_x().wait_recv()
    pb_x().wait_recv()
    for g in range(Gd):
        pbt[g] = jnp.concatenate([pbs[g], pbr[g]], axis=0).T.astype(BF16)
    px_own.wait()

    def heard(j, carry):
        tot_copy(j, j).wait_recv()
        return carry

    lax.fori_loop(me + 1, 2 * R, heard, 0)

    slot = lax.broadcasted_iota(jnp.int32, tots.shape, 0)
    every = tots[...]
    after_me = jnp.sum(jnp.where(slot > me, every, 0.0), axis=0)[0:1, :]
    after_other = jnp.sum(jnp.where(slot > other, every, 0.0), axis=0)[0:1, :]
    w2[:tok, :H] = us[...] * jnp.exp(after_me)
    w2[tok:, :H] = ur[...] * jnp.exp(after_other)

    def produce(k):
        base = place(s, k)

        @pl.when(k % PER == 0)
        def _():
            px_x(k // PER).wait_recv()

        at = pl.ds(pl.multiple_of((k % PER) * WIDTH, WIDTH), block)
        mine = pxv[:, pl.ds(base, block)].astype(F32) * spread(w2[:tok], base, block)
        theirs = pxr[k // PER, :, at] * spread(w2[tok:], base, block)
        scaled = jnp.concatenate([mine, theirs], axis=0).astype(BF16)
        state = dot(pbt[base // gw], scaled)
        for q in range(PAIR):
            for v in range(SPLIT):
                s_own[(k + q) * SPLIT + v] = state[
                    v * ROWS : (v + 1) * ROWS, q * WIDTH : (q + 1) * WIDTH
                ]

    right = {"req": jnp.minimum(i + 1, R - 1)}
    left = {"req": jnp.maximum(i - 1, 0)}

    def l_copy(src, dst, up, k):
        return remote(src, dst, l_send.at[up], l_recv.at[k], right)

    def r_copy(src, dst, up, k):
        return remote(src, dst, r_send.at[up], r_recv.at[k], left)

    def state_l(k):
        return l_copy(s_lout.at[k], s_lin.at[k], 0, k % DEEP)

    def own_l(k):
        return l_copy(s_own.at[k], s_lin.at[k], 0, k % DEEP)

    def state_r(k):
        return r_copy(s_rout.at[k], s_rin.at[k], 0, k % DEEP)

    def own_r(k):
        return r_copy(s_own.at[k], s_rin.at[k], 0, k % DEEP)

    def carry_l():
        return l_copy(c_lout, c_lin, 1, DEEP)

    def own_carry_l():
        return l_copy(c_own, c_lin, 1, DEEP)

    def carry_r():
        return r_copy(c_rout, c_rin, 1, DEEP)

    def own_carry_r():
        return r_copy(c_own, c_rin, 1, DEEP)

    def carry_a():
        return remote(c_tot, c_ag, a_send.at[1], a_recv.at[RING], sib)

    def state_a(k):
        rows = pl.ds(k * SPLIT, SPLIT)
        return remote(
            s_tot.at[rows], s_ag.at[rows], a_send.at[0], a_recv.at[k // PAIR % RING], sib
        )

    def pair_a(k):
        rows = pl.ds(k * SPLIT, RUN)
        return remote(
            s_tot.at[rows], s_ag.at[rows], a_send.at[0], a_recv.at[k // PAIR % RING], sib
        )

    def z_copy(j):
        rows = pl.ds(j, QUAD)
        return remote(st0.at[rows], st0.at[rows], z_send.at[0], z_recv.at[j // OCT], sib)

    def oct_z(j):
        rows = pl.ds(j, OCT)
        return remote(st0.at[rows], st0.at[rows], z_send.at[0], z_recv.at[j // OCT], sib)

    def push(source, sink, own, came, out_ref, relay, straight):
        @pl.when(source)
        def _():
            straight().start()

        @pl.when(jnp.logical_not(source))
        def _():
            relay().wait_recv()

            @pl.when(jnp.logical_not(sink))
            def _():
                out_ref[...] = own[...] + came[...]
                relay().start()

    def close(own, lin, lout, rin, tot):
        @pl.when(first)
        def _():
            tot[...] = own[...] + rin[...]

        @pl.when(last)
        def _():
            tot[...] = own[...] + lin[...]

        @pl.when(jnp.logical_not(first | last))
        def _():
            tot[...] = lout[...] + rin[...]

    def cont_chunk(owner, k):
        base = place(owner, k)
        j = owner * K + k
        at = pl.ds(base, wide_block)
        steered = (cxv[:, at].astype(F32) + mv[:, at]).astype(BF16)
        wide = steered.astype(F32)
        out[:, at] = skc[0:1, at] * wide
        scaled = (wide * spread(colw[...], base, wide_block)).astype(BF16)
        for q in range(QUAD):
            sc[j + q] = scaled[:, q * WIDTH : (q + 1) * WIDTH]

        @pl.when(s == 0)
        def _():
            state = dot(cbt[base // gw], scaled)
            for q in range(QUAD):
                st0[j + q] = state[:, q * WIDTH : (q + 1) * WIDTH]
            z_copy(j).start()

    def finish(owner, k, ready):
        base = place(owner, k)
        j = owner * K + k
        at = pl.ds(base, block)
        coming = jnp.concatenate(
            [
                jnp.concatenate([ready[(k + q) * SPLIT + v] for v in range(SPLIT)], axis=0)
                for q in range(PAIR)
            ],
            axis=1,
        )
        before = jnp.concatenate([st0[j + q] for q in range(PAIR)], axis=1)
        start = coming + spread(carw[...], base, block) * mv[:, at]
        incoming = ((start + second * before) * fc[0:1, at]).astype(BF16)
        scaled = jnp.concatenate([sc[j + q] for q in range(PAIR)], axis=1)
        z = dot(gc[base // gw], jnp.concatenate([scaled, incoming], axis=0))
        mixed = out[:, at] + spread(roww[...], base, block) * z
        out[:, at] = mixed * gav[:, at]
        square = mixed * mixed
        folded = square[:, :LANES]
        for q in range(1, block // LANES):
            folded = folded + square[:, q * LANES : (q + 1) * LANES]
        return folded

    def within(k):
        return (k >= 0) & (k < U)

    second = jnp.where(s == 1, 1.0, 0.0).astype(F32)
    for k in range(0, AHEAD, PAIR):
        produce(jnp.int32(k))

        @pl.when(first)
        def _():
            for q in range(RUN):
                own_l(jnp.int32(k * SPLIT + q)).start()

        @pl.when(last)
        def _():
            for q in range(RUN):
                own_r(jnp.int32(k * SPLIT + q)).start()

    def sum_carry():
        lane_group = lax.broadcasted_iota(jnp.int32, (nh, H), 1)
        carry = jnp.zeros((nh, H), F32)
        weight = thirds(w2[:, :H])
        rows = pl.ds(pl.multiple_of(s * nh, nh), nh)
        for g in range(Gd):
            inside = (lane_group >= g * per_group) & (lane_group < (g + 1) * per_group)
            part = dot(jnp.concatenate([pbt[g, rows]] * 3, axis=1), weight)
            carry = jnp.where(inside, part, carry)
        c_own[...] = carry

    def cont_decays():
        cdt_in.wait()
        ccum = running_sum(-rav[...] * cdv[...])
        ctot[...] = jnp.broadcast_to(ccum[T - 1 :, :], (8, H))

        @pl.when(s == 0)
        def _():
            d_copy().start()

        colw[:, :H] = jnp.exp(-ccum) * cdv[...]
        roww[:, :H] = jnp.exp(ccum)
        ssacc[...] = jnp.zeros_like(ssacc)

    def row_of(value, to):
        value = padded(jnp.broadcast_to(value, (8, H)))
        lane = lax.broadcasted_iota(jnp.int32, (8, LANES), 1)
        for q in range(C // LANES):
            at = lax.shift_right_logical(lane, head.bit_length() - 1) + q * (LANES // head)
            to[:, q * LANES : (q + 1) * LANES] = jnp.take_along_axis(
                value, at, axis=1, mode="promise_in_bounds"
            )

    def channel_rows():
        for copy in later:
            copy.wait()
        entry = lax.broadcasted_iota(jnp.int32, tav.shape, 1) == mult_at[0]
        multiplier = jnp.sum(jnp.where(entry, tav[...], 0.0), axis=1, keepdims=True)
        wanted = lax.broadcasted_iota(jnp.int32, vecs.shape, 0) == behav_at[0]
        mv[...] = multiplier * jnp.sum(jnp.where(wanted, vev[...], 0.0), axis=0, keepdims=True)
        row_of(skv[...], skc)

        @pl.when(s == 0)
        def _():
            fc[...] = jnp.ones_like(fc)

        @pl.when(s == 1)
        def _():
            d_copy().wait_recv()
            row_of(jnp.exp(ctot_in[0:1, :]), fc)

    def group_products(g):
        lower = lax.broadcasted_iota(jnp.int32, (T, T), 0) >= lax.broadcasted_iota(
            jnp.int32, (T, T), 1
        )
        bmat = cbv[:, 0, g, :].astype(F32)
        cmat = cbv[:, 1, g, :].astype(F32).astype(BF16)
        cbt[g] = bmat.T.astype(BF16)
        gmat = jnp.where(lower, dot_t(cmat, bmat.astype(BF16)), 0.0)
        gc[g] = jnp.concatenate([gmat.astype(BF16), cmat], axis=1)

    cbc_in.wait()
    cx_in.wait()

    def step(m, unused):
        kl = m - SKEW_L * i
        kr = m - SKEW_R * hr
        kt = m - far
        kf = kt - RUN // 2

        @pl.when(within(kr) & ((kr >= BEFORE) | (hr > 0)))
        def _():
            push(
                last,
                first,
                s_own.at[kr],
                s_rin.at[kr],
                s_rout.at[kr],
                functools.partial(state_r, kr),
                functools.partial(own_r, kr),
            )

        @pl.when(within(kl) & ((kl >= BEFORE) | (i > 0)))
        def _():
            push(
                first,
                last,
                s_own.at[kl],
                s_lin.at[kl],
                s_lout.at[kl],
                functools.partial(state_l, kl),
                functools.partial(own_l, kl),
            )

        @pl.when(kr == TURN)
        def _():
            push(last, first, c_own, c_rin, c_rout, carry_r, own_carry_r)

        @pl.when(kl == TURN)
        def _():
            push(first, last, c_own, c_lin, c_lout, carry_l, own_carry_l)

        @pl.when(within(kt))
        def _():
            close(s_own.at[kt], s_lin.at[kt], s_lout.at[kt], s_rin.at[kt], s_tot.at[kt])

        @pl.when(within(kt) & (kt % SPLIT == SPLIT - 1))
        def _():
            state_a(kt // SPLIT).start()

        @pl.when(kt == TURN)
        def _():
            close(c_own, c_lin, c_lout, c_rin, c_tot)
            carry_a().start()

        @pl.when((m % RUN == 0) & (m + BEFORE < U))
        def _():
            produce(m // SPLIT + AHEAD)

        for number, work in enumerate((sum_carry, cont_decays, channel_rows)):
            pl.when(m == number)(work)

        for g in range(Gd):
            pl.when(m == g % SETUP)(functools.partial(group_products, g))

        spent = m - SETUP

        @pl.when((spent >= 0) & (spent % SPLIT == 0) & (spent < SPLIT * (2 * K // QUAD)))
        def _():
            turn = spent // SPLIT
            cont_chunk(jnp.where(turn % 2 == 0, s, 1 - s), turn // 2 * QUAD)

        @pl.when(kt == TURN + SPLIT)
        def _():
            carry_a().wait_recv()

            @pl.when(s == 1)
            def _():
                oct_z(0).wait_recv()
                oct_z(K).wait_recv()

            carw[pl.ds(pl.multiple_of(s * nh, nh), nh), :H] = c_tot[...]
            carw[pl.ds(pl.multiple_of((1 - s) * nh, nh), nh), :H] = c_ag[...]

        @pl.when((kt > TURN) & (kt < U) & (kt % RUN == RUN - 1))
        def _():
            k = kt // SPLIT - PAIR + 1

            @pl.when((s == 1) & (k % OCT == 0))
            def _():
                oct_z(k).wait_recv()
                oct_z(k + K).wait_recv()

            ssacc[...] += finish(s, k, s_tot)

        @pl.when((kf > TURN) & (kf < U) & (kf % RUN == RUN - 1))
        def _():
            k = kf // SPLIT - PAIR + 1
            pair_a(k).wait_recv()
            ssacc[...] += finish(1 - s, k, s_ag)

        @pl.when((kt >= 2 * TURN) & (kt < 3 * TURN) & (kt % RUN == 0))
        def _():
            k = (kt - 2 * TURN) // SPLIT
            ssacc[...] += finish(s, k, s_tot)
            pair_a(k).wait_recv()
            ssacc[...] += finish(1 - s, k, s_ag)

        return unused

    steps = U + max(SKEW_L, SKEW_R) * (R - 1) + RUN // 2
    lax.fori_loop(0, steps, step, 0)

    folded = ssacc[...].T
    partial = folded[0:8]
    for q in range(1, LANES // 8):
        partial = partial + folded[q * 8 : (q + 1) * 8]
    ssl[x] = partial

    def p_copy(j, at):
        return remote(ssl.at[at], ssl.at[at], p_send.at[j], p_recv.at[at], {"tp": j})

    each(TP, x, lambda j: p_copy(j, x).start())

    x_copy(pxs, pxr, 0, 0).wait_send()
    remote(s_tot, s_ag, a_send.at[0], a_recv.at[0], sib).wait_send()
    u_x().wait_send()
    pb_x().wait_send()
    carry_a().wait_send()

    @pl.when(jnp.logical_not(last))
    def _():
        carry_l().wait_send()
        l_copy(s_lout, s_lin, 0, 0).wait_send()

    @pl.when(jnp.logical_not(first))
    def _():
        carry_r().wait_send()
        r_copy(s_rout, s_rin, 0, 0).wait_send()

    @pl.when(s == 0)
    def _():
        d_copy().wait_send()
        remote(st0, st0, z_send.at[0], z_recv.at[0], sib).wait_send()

    def told(j, carry):
        tot_copy(j, me).wait_send()
        return carry

    lax.fori_loop(0, me, told, 0)


    each(TP, x, lambda j: p_copy(j, j).wait_recv())
    meansq = jnp.sum(jnp.sum(ssl[...], axis=0), axis=0, keepdims=True) / (C * TP)
    scale_out[...] = jnp.broadcast_to(lax.rsqrt(meansq + 1e-05), scale_out.shape)
    each(TP, x, lambda j: p_copy(j, x).wait_send())


def local(
    prompt_x,
    prompt_b,
    prompt_dt,
    cont_x,
    cont_bc,
    cont_dt,
    decay_rate,
    skip_gain,
    norm_gain,
    steer_vecs,
    mult_table,
    mult_idx,
    behav_idx,
):
    R, TP = lax.axis_size("req"), lax.axis_size("tp")
    H = decay_rate.shape[0]
    tok, C = prompt_x.shape
    Gd, N = prompt_b.shape[1:]
    T = cont_x.shape[1]
    K = C // 2 // WIDTH
    NX = C // 2 // PIECE
    HP = max(H, LANES)
    DEEP = min(K * SPLIT, (R - 1) * max(SKEW_L, SKEW_R) + 2)
    def outside_of(*values):
        return tuple(pltpu.with_memory_space_constraint(v, pltpu.HBM) for v in values)

    args = outside_of(
        prompt_x,
        prompt_b,
        prompt_dt,
        cont_x[0],
        cont_bc[0],
        cont_dt[0],
        decay_rate[None],
        skip_gain[None],
        norm_gain[None],
        steer_vecs,
        mult_table[None],
    ) + (mult_idx, behav_idx)
    vmem, dma = pltpu.VMEM, pltpu.SemaphoreType.DMA
    inside = pl.BlockSpec(memory_space=pltpu.VMEM)
    outside = pl.BlockSpec(memory_space=pl.ANY)
    scalars = pl.BlockSpec(memory_space=pltpu.SMEM)
    part = (K * SPLIT, N // SPLIT, WIDTH)
    carried = (N // 2, H)
    scratch = (
        [
            vmem((tok, H), F32),
            vmem((tok, Gd, N), BF16),
            vmem((1, H), F32),
            vmem((1, H), F32),
            vmem((1, C), F32),
            vmem((1, mult_table.shape[0]), F32),
            vmem((tok, C), BF16),
            vmem((T, C), BF16),
            vmem(cont_bc.shape[1:], BF16),
            vmem((T, H), F32),
            vmem(steer_vecs.shape, F32),
        ]
        + [vmem((NX, tok, PIECE), F32)] * 2
        + [vmem((tok, H), F32)] * 2
        + [vmem((Gd, tok, N), F32)] * 2
        + [vmem((Gd, N, 2 * tok), BF16)]
        + [vmem((2 * tok, HP), F32)]
        + [vmem((T, HP), F32)] * 2
        + [vmem((Gd, T, T + N), BF16), vmem((Gd, N, T), BF16)]
        + [vmem((1, C), F32), vmem((8, C), F32), vmem((8, C), F32)]
        + [vmem((2 * R, 8, H), F32)]
        + [vmem((8, H), F32)] * 2
        + [vmem((2 * K, T, WIDTH), BF16)]
        + [vmem((2 * K, N, WIDTH), F32)]
        + [vmem(part, F32)] * 7
        + [vmem(carried, F32)] * 7
        + [vmem((N, HP), F32), vmem((T, LANES), F32), vmem((TP, 8, T), F32)]
        + [dma((NX + 11,))]
        + [dma((2 * R,))] * 2
        + [dma((3,)), dma((NX + 2,))]
        + [dma((2,)), dma((DEEP + 1,))] * 2
        + [dma((2,)), dma((RING + 1,))]
        + [dma((1,)), dma((2 * K // OCT,))]
        + [dma((1,))] * 2
        + [dma((TP,))] * 2
    )
    mixed, scale = pl.pallas_call(
        functools.partial(kernel, R, TP, K, HP, DEEP),
        out_shape=[jax.ShapeDtypeStruct((T, C), F32), jax.ShapeDtypeStruct((8, T), F32)],
        in_specs=[outside] * 11 + [scalars] * 2,
        out_specs=[inside, inside],
        scratch_shapes=scratch,
        compiler_params=pltpu.CompilerParams(
            collective_id=0, has_side_effects=True, vmem_limit_bytes=40 * 1024 * 1024
        ),
        name="sweep",
    )(*args)
    return (mixed * scale[0][:, None]).astype(BF16)[None]


def solution(mesh):
    return jax.shard_map(
        local,
        mesh=mesh,
        in_specs=(
            P(("parts", "req", "sp"), "tp"),
            P(("parts", "req", "sp"), "tp", None),
            P(("parts", "req", "sp"), "tp"),
            P(("parts", "req"), "sp", "tp"),
            P(("parts", "req"), "sp", None, "tp", None),
            P(("parts", "req"), "sp", "tp"),
            P("tp"),
            P("tp"),
            P("tp"),
            P(None, "tp"),
            P(),
            P(("parts", "req")),
            P(("parts", "req")),
        ),
        out_specs=P(("parts", "req"), "sp", "tp"),
        check_vma=False,
    )
```

```python
import functools

import jax
import jax.numpy as jnp
from jax import lax
from jax.experimental import pallas as pl
from jax.experimental.pallas import tpu as pltpu
from jax.sharding import PartitionSpec as P

MESH = pl.DeviceIdType.MESH
F32 = jnp.float32
BF16 = jnp.bfloat16
LANES = 128
WIDTH = 128
SPLIT = 1
PAIR = 2
QUAD = 4
OCT = 4
PIECE = 1024
RING = 8
TURN = 4 * SPLIT
SETUP = 4
AHEAD = 4
SKEW_L = 3
SKEW_R = 2


def dot(a, b):
    return jnp.dot(a, b, preferred_element_type=F32)


def dot_t(a, b):
    return lax.dot_general(a, b, (((1,), (1,)), ((), ())), preferred_element_type=F32)


def thirds(value):
    lead = value.astype(BF16)
    rest = value - lead.astype(F32)
    mid = rest.astype(BF16)
    low = (rest - mid.astype(F32)).astype(BF16)
    return jnp.concatenate([lead, mid, low], axis=0)


def running_sum(rows):
    length = rows.shape[0]
    lower = lax.broadcasted_iota(jnp.int32, (length, length), 0) >= lax.broadcasted_iota(
        jnp.int32, (length, length), 1
    )
    ones = jnp.where(lower, 1.0, 0.0).astype(BF16)
    return dot(jnp.concatenate([ones] * 3, axis=1), thirds(rows))


def kernel(
    R,
    TP,
    K,
    HP,
    DEEP,
    px,
    pb,
    pdt,
    cx,
    cbc,
    cdt,
    rate,
    skip,
    gain,
    vecs,
    table,
    mult_at,
    behav_at,
    out,
    scale_out,
    pdv,
    pbv,
    rav,
    skv,
    gav,
    tav,
    pxv,
    cxv,
    cbv,
    cdv,
    vev,
    pxs,
    pxr,
    us,
    ur,
    pbs,
    pbr,
    pbt,
    w2,
    colw,
    roww,
    gc,
    cbt,
    mv,
    skc,
    fc,
    tots,
    ctot,
    ctot_in,
    sc,
    st0,
    s_own,
    s_lin,
    s_lout,
    s_rin,
    s_rout,
    s_tot,
    s_ag,
    c_own,
    c_lin,
    c_lout,
    c_rin,
    c_rout,
    c_tot,
    c_ag,
    carw,
    ssacc,
    ssl,
    h_sem,
    t_send,
    t_recv,
    x_send,
    x_recv,
    l_send,
    l_recv,
    r_send,
    r_recv,
    a_send,
    a_recv,
    z_send,
    z_recv,
    d_send,
    d_recv,
    p_send,
    p_recv,
):
    i = lax.axis_index("req")
    s = lax.axis_index("sp")
    x = lax.axis_index("tp")
    me = i * 2 + s
    other = i * 2 + 1 - s
    hr = R - 1 - i
    far = jnp.maximum(SKEW_L * i, SKEW_R * hr)
    tok, H = pdt.shape
    block = WIDTH * PAIR
    wide_block = WIDTH * QUAD

    C = px.shape[1]
    Gd, N = pb.shape[1:]
    T = cx.shape[0]
    U = K * SPLIT
    ROWS = N // SPLIT
    RUN = PAIR * SPLIT
    BEFORE = AHEAD * SPLIT
    half = C // 2
    head = C // H
    gw = C // Gd
    per_group = H // Gd
    nh = N // 2
    NX = half // PIECE
    PER = PIECE // WIDTH
    sib = {"sp": 1 - s}
    first, last = i == 0, i == R - 1

    def each(count, skip_index, body):
        def turn(j, carry):
            @pl.when(j != skip_index)
            def _():
                body(j)

            return carry

        lax.fori_loop(0, count, turn, 0)

    def peer(j):
        return {"req": j // 2, "sp": j % 2}

    def remote(src, dst, send, recv, device):
        return pltpu.make_async_remote_copy(
            src_ref=src,
            dst_ref=dst,
            send_sem=send,
            recv_sem=recv,
            device_id=device,
            device_id_type=MESH,
        )

    def h_copy(src, dst, k):
        return pltpu.make_async_copy(src, dst, h_sem.at[k])

    def piece_at(owner, q):
        return pl.ds(pl.multiple_of(owner * half + q * PIECE, PIECE), PIECE)

    own_half = pl.ds(pl.multiple_of(s * half, half), half)
    pieces = [
        h_copy(px.at[:, piece_at(1 - s, q)], pxv.at[:, piece_at(1 - s, q)], q) for q in range(NX)
    ]
    early = [h_copy(pdt, pdv, NX), h_copy(rate, rav, NX + 1), h_copy(pb, pbv, NX + 2)]
    px_own = h_copy(px.at[:, own_half], pxv.at[:, own_half], NX + 3)
    cdt_in = h_copy(cdt, cdv, NX + 4)
    cbc_in = h_copy(cbc, cbv, NX + 5)
    later = [
        h_copy(vecs, vev, NX + 6),
        h_copy(table, tav, NX + 7),
        h_copy(skip, skv, NX + 8),
        h_copy(gain, gav, NX + 9),
    ]
    cx_in = h_copy(cx, cxv, NX + 10)
    barrier = pltpu.get_barrier_semaphore()

    def greet(j, carry):
        @pl.when((j > me) | (j == other) | (j == me - 2))
        def _():
            pl.semaphore_signal(barrier, inc=1, device_id=peer(j), device_id_type=MESH)

        return carry

    lax.fori_loop(0, 2 * R, greet, 0)
    each(
        TP,
        x,
        lambda j: pl.semaphore_signal(barrier, inc=1, device_id={"tp": j}, device_id_type=MESH),
    )
    for copy in pieces[:1] + early + pieces[1:]:
        copy.start()
    for copy in [px_own, cdt_in, cbc_in] + later + [cx_in]:
        copy.start()

    pieces[0].wait()
    pxs[0] = pxv[:, piece_at(1 - s, 0)].astype(F32)
    early[2].wait()
    for g in range(Gd):
        pbs[g] = pbv[:, g, :].astype(F32)
    greeted = me + (1 - s) + jnp.where(i < R - 1, 1, 0) + TP - 1
    pl.semaphore_wait(barrier, greeted)

    def tot_copy(j, slot):
        return remote(tots.at[slot], tots.at[slot], t_send.at[j], t_recv.at[slot], peer(j))

    def x_copy(src, dst, up, k):
        return remote(src, dst, x_send.at[up], x_recv.at[k], sib)

    def px_x(q):
        return x_copy(pxs.at[q], pxr.at[q], 0, q)

    def u_x():
        return x_copy(us, ur, 1, NX)

    def pb_x():
        return x_copy(pbs, pbr, 2, NX + 1)

    def d_copy():
        return remote(ctot, ctot_in, d_send.at[0], d_recv.at[0], sib)

    px_x(0).start()
    pb_x().start()
    early[0].wait()
    early[1].wait()
    cum = running_sum(-rav[...] * pdv[...])
    total = cum[tok - 1 :, :]
    tots[me] = jnp.broadcast_to(total, (8, H))
    us[...] = jnp.exp(total - cum) * pdv[...]
    u_x().start()

    def tell(j, carry):
        tot_copy(j, me).start()
        return carry

    lax.fori_loop(0, me, tell, 0)

    for q in range(1, NX):
        pieces[q].wait()
        pxs[q] = pxv[:, piece_at(1 - s, q)].astype(F32)
        px_x(q).start()

    def padded(value):
        return jnp.concatenate([value] * (HP // H), axis=1) if HP > H else value

    def spread(value, base, width):
        lane = lax.broadcasted_iota(jnp.int32, (value.shape[0], LANES), 1)
        shift = head.bit_length() - 1
        parts = []
        for q in range(width // LANES):
            at = lax.shift_right_logical(lane, shift) + (base // head + q * (LANES // head))
            parts.append(jnp.take_along_axis(value, at, axis=1, mode="promise_in_bounds"))
        return parts[0] if len(parts) == 1 else jnp.concatenate(parts, axis=1)

    def place(owner, k):
        return pl.multiple_of(owner * half + k * WIDTH, WIDTH)

    u_x().wait_recv()
    pb_x().wait_recv()
    for g in range(Gd):
        pbt[g] = jnp.concatenate([pbs[g], pbr[g]], axis=0).T.astype(BF16)
    px_own.wait()

    def heard(j, carry):
        tot_copy(j, j).wait_recv()
        return carry

    lax.fori_loop(me + 1, 2 * R, heard, 0)

    slot = lax.broadcasted_iota(jnp.int32, tots.shape, 0)
    every = tots[...]
    after_me = jnp.sum(jnp.where(slot > me, every, 0.0), axis=0)[0:1, :]
    after_other = jnp.sum(jnp.where(slot > other, every, 0.0), axis=0)[0:1, :]
    w2[:tok, :H] = us[...] * jnp.exp(after_me)
    w2[tok:, :H] = ur[...] * jnp.exp(after_other)

    def produce(k):
        base = place(s, k)

        @pl.when(k % PER == 0)
        def _():
            px_x(k // PER).wait_recv()

        at = pl.ds(pl.multiple_of((k % PER) * WIDTH, WIDTH), block)
        mine = pxv[:, pl.ds(base, block)].astype(F32) * spread(w2[:tok], base, block)
        theirs = pxr[k // PER, :, at] * spread(w2[tok:], base, block)
        scaled = jnp.concatenate([mine, theirs], axis=0).astype(BF16)
        state = dot(pbt[base // gw], scaled)
        for q in range(PAIR):
            for v in range(SPLIT):
                s_own[(k + q) * SPLIT + v] = state[
                    v * ROWS : (v + 1) * ROWS, q * WIDTH : (q + 1) * WIDTH
                ]

    right = {"req": jnp.minimum(i + 1, R - 1)}
    left = {"req": jnp.maximum(i - 1, 0)}

    def l_copy(src, dst, up, k):
        return remote(src, dst, l_send.at[up], l_recv.at[k], right)

    def r_copy(src, dst, up, k):
        return remote(src, dst, r_send.at[up], r_recv.at[k], left)

    def state_l(k):
        return l_copy(s_lout.at[k], s_lin.at[k], 0, k % DEEP)

    def own_l(k):
        return l_copy(s_own.at[k], s_lin.at[k], 0, k % DEEP)

    def state_r(k):
        return r_copy(s_rout.at[k], s_rin.at[k], 0, k % DEEP)

    def own_r(k):
        return r_copy(s_own.at[k], s_rin.at[k], 0, k % DEEP)

    def carry_l():
        return l_copy(c_lout, c_lin, 1, DEEP)

    def own_carry_l():
        return l_copy(c_own, c_lin, 1, DEEP)

    def carry_r():
        return r_copy(c_rout, c_rin, 1, DEEP)

    def own_carry_r():
        return r_copy(c_own, c_rin, 1, DEEP)

    def carry_a():
        return remote(c_tot, c_ag, a_send.at[1], a_recv.at[RING], sib)

    def state_a(k):
        rows = pl.ds(k * SPLIT, SPLIT)
        return remote(
            s_tot.at[rows], s_ag.at[rows], a_send.at[0], a_recv.at[k // PAIR % RING], sib
        )

    def pair_a(k):
        rows = pl.ds(k * SPLIT, RUN)
        return remote(
            s_tot.at[rows], s_ag.at[rows], a_send.at[0], a_recv.at[k // PAIR % RING], sib
        )

    def z_copy(j):
        rows = pl.ds(j, QUAD)
        return remote(st0.at[rows], st0.at[rows], z_send.at[0], z_recv.at[j // OCT], sib)

    def oct_z(j):
        rows = pl.ds(j, OCT)
        return remote(st0.at[rows], st0.at[rows], z_send.at[0], z_recv.at[j // OCT], sib)

    def push(source, sink, own, came, out_ref, relay, straight):
        @pl.when(source)
        def _():
            straight().start()

        @pl.when(jnp.logical_not(source))
        def _():
            relay().wait_recv()

            @pl.when(jnp.logical_not(sink))
            def _():
                out_ref[...] = own[...] + came[...]
                relay().start()

    def close(own, lin, lout, rin, tot):
        @pl.when(first)
        def _():
            tot[...] = own[...] + rin[...]

        @pl.when(last)
        def _():
            tot[...] = own[...] + lin[...]

        @pl.when(jnp.logical_not(first | last))
        def _():
            tot[...] = lout[...] + rin[...]

    def cont_chunk(owner, k):
        base = place(owner, k)
        j = owner * K + k
        at = pl.ds(base, wide_block)
        steered = (cxv[:, at].astype(F32) + mv[:, at]).astype(BF16)
        wide = steered.astype(F32)
        out[:, at] = skc[0:1, at] * wide
        scaled = (wide * spread(colw[...], base, wide_block)).astype(BF16)
        for q in range(QUAD):
            sc[j + q] = scaled[:, q * WIDTH : (q + 1) * WIDTH]

        @pl.when(s == 0)
        def _():
            state = dot(cbt[base // gw], scaled)
            for q in range(QUAD):
                st0[j + q] = state[:, q * WIDTH : (q + 1) * WIDTH]
            z_copy(j).start()

    def finish(owner, k, ready):
        base = place(owner, k)
        j = owner * K + k
        at = pl.ds(base, block)
        coming = jnp.concatenate(
            [
                jnp.concatenate([ready[(k + q) * SPLIT + v] for v in range(SPLIT)], axis=0)
                for q in range(PAIR)
            ],
            axis=1,
        )
        before = jnp.concatenate([st0[j + q] for q in range(PAIR)], axis=1)
        start = coming + spread(carw[...], base, block) * mv[:, at]
        incoming = ((start + second * before) * fc[0:1, at]).astype(BF16)
        scaled = jnp.concatenate([sc[j + q] for q in range(PAIR)], axis=1)
        z = dot(gc[base // gw], jnp.concatenate([scaled, incoming], axis=0))
        mixed = out[:, at] + spread(roww[...], base, block) * z
        out[:, at] = mixed * gav[:, at]
        square = mixed * mixed
        folded = square[:, :LANES]
        for q in range(1, block // LANES):
            folded = folded + square[:, q * LANES : (q + 1) * LANES]
        return folded

    def within(k):
        return (k >= 0) & (k < U)

    second = jnp.where(s == 1, 1.0, 0.0).astype(F32)
    for k in range(0, AHEAD, PAIR):
        produce(jnp.int32(k))

        @pl.when(first)
        def _():
            for q in range(RUN):
                own_l(jnp.int32(k * SPLIT + q)).start()

        @pl.when(last)
        def _():
            for q in range(RUN):
                own_r(jnp.int32(k * SPLIT + q)).start()

    def sum_carry():
        lane_group = lax.broadcasted_iota(jnp.int32, (nh, H), 1)
        carry = jnp.zeros((nh, H), F32)
        weight = thirds(w2[:, :H])
        rows = pl.ds(pl.multiple_of(s * nh, nh), nh)
        for g in range(Gd):
            inside = (lane_group >= g * per_group) & (lane_group < (g + 1) * per_group)
            part = dot(jnp.concatenate([pbt[g, rows]] * 3, axis=1), weight)
            carry = jnp.where(inside, part, carry)
        c_own[...] = carry

    def cont_decays():
        cdt_in.wait()
        ccum = running_sum(-rav[...] * cdv[...])
        ctot[...] = jnp.broadcast_to(ccum[T - 1 :, :], (8, H))

        @pl.when(s == 0)
        def _():
            d_copy().start()

        colw[:, :H] = jnp.exp(-ccum) * cdv[...]
        roww[:, :H] = jnp.exp(ccum)
        ssacc[...] = jnp.zeros_like(ssacc)

    def row_of(value, to):
        value = padded(jnp.broadcast_to(value, (8, H)))
        lane = lax.broadcasted_iota(jnp.int32, (8, LANES), 1)
        for q in range(C // LANES):
            at = lax.shift_right_logical(lane, head.bit_length() - 1) + q * (LANES // head)
            to[:, q * LANES : (q + 1) * LANES] = jnp.take_along_axis(
                value, at, axis=1, mode="promise_in_bounds"
            )

    def channel_rows():
        for copy in later:
            copy.wait()
        entry = lax.broadcasted_iota(jnp.int32, tav.shape, 1) == mult_at[0]
        multiplier = jnp.sum(jnp.where(entry, tav[...], 0.0), axis=1, keepdims=True)
        wanted = lax.broadcasted_iota(jnp.int32, vecs.shape, 0) == behav_at[0]
        mv[...] = multiplier * jnp.sum(jnp.where(wanted, vev[...], 0.0), axis=0, keepdims=True)
        row_of(skv[...], skc)

        @pl.when(s == 0)
        def _():
            fc[...] = jnp.ones_like(fc)

        @pl.when(s == 1)
        def _():
            d_copy().wait_recv()
            row_of(jnp.exp(ctot_in[0:1, :]), fc)

    def group_products(g):
        lower = lax.broadcasted_iota(jnp.int32, (T, T), 0) >= lax.broadcasted_iota(
            jnp.int32, (T, T), 1
        )
        bmat = cbv[:, 0, g, :].astype(F32)
        cmat = cbv[:, 1, g, :].astype(F32).astype(BF16)
        cbt[g] = bmat.T.astype(BF16)
        gmat = jnp.where(lower, dot_t(cmat, bmat.astype(BF16)), 0.0)
        gc[g] = jnp.concatenate([gmat.astype(BF16), cmat], axis=1)

    cbc_in.wait()
    cx_in.wait()

    def step(m, unused):
        kl = m - SKEW_L * i
        kr = m - SKEW_R * hr
        kt = m - far
        kf = kt - RUN // 2

        @pl.when(within(kr) & ((kr >= BEFORE) | (hr > 0)))
        def _():
            push(
                last,
                first,
                s_own.at[kr],
                s_rin.at[kr],
                s_rout.at[kr],
                functools.partial(state_r, kr),
                functools.partial(own_r, kr),
            )

        @pl.when(within(kl) & ((kl >= BEFORE) | (i > 0)))
        def _():
            push(
                first,
                last,
                s_own.at[kl],
                s_lin.at[kl],
                s_lout.at[kl],
                functools.partial(state_l, kl),
                functools.partial(own_l, kl),
            )

        @pl.when(kr == TURN)
        def _():
            push(last, first, c_own, c_rin, c_rout, carry_r, own_carry_r)

        @pl.when(kl == TURN)
        def _():
            push(first, last, c_own, c_lin, c_lout, carry_l, own_carry_l)

        @pl.when(within(kt))
        def _():
            close(s_own.at[kt], s_lin.at[kt], s_lout.at[kt], s_rin.at[kt], s_tot.at[kt])

        @pl.when(within(kt) & (kt % SPLIT == SPLIT - 1))
        def _():
            state_a(kt // SPLIT).start()

        @pl.when(kt == TURN)
        def _():
            close(c_own, c_lin, c_lout, c_rin, c_tot)
            carry_a().start()

        @pl.when((m % RUN == 0) & (m + BEFORE < U))
        def _():
            produce(m // SPLIT + AHEAD)

        for number, work in enumerate((sum_carry, cont_decays, channel_rows)):
            pl.when(m == number)(work)

        for g in range(Gd):
            pl.when(m == g % SETUP)(functools.partial(group_products, g))

        spent = m - SETUP

        @pl.when((spent >= 0) & (spent % SPLIT == 0) & (spent < SPLIT * (2 * K // QUAD)))
        def _():
            turn = spent // SPLIT
            cont_chunk(jnp.where(turn % 2 == 0, s, 1 - s), turn // 2 * QUAD)

        @pl.when(kt == TURN + SPLIT)
        def _():
            carry_a().wait_recv()

            @pl.when(s == 1)
            def _():
                oct_z(0).wait_recv()
                oct_z(K).wait_recv()

            carw[pl.ds(pl.multiple_of(s * nh, nh), nh), :H] = c_tot[...]
            carw[pl.ds(pl.multiple_of((1 - s) * nh, nh), nh), :H] = c_ag[...]

        @pl.when((kt > TURN) & (kt < U) & (kt % RUN == RUN - 1))
        def _():
            k = kt // SPLIT - PAIR + 1

            @pl.when((s == 1) & (k % OCT == 0))
            def _():
                oct_z(k).wait_recv()
                oct_z(k + K).wait_recv()

            ssacc[...] += finish(s, k, s_tot)

        @pl.when((kf > TURN) & (kf < U) & (kf % RUN == RUN - 1))
        def _():
            k = kf // SPLIT - PAIR + 1
            pair_a(k).wait_recv()
            ssacc[...] += finish(1 - s, k, s_ag)

        @pl.when((kt >= 2 * TURN) & (kt < 3 * TURN) & (kt % RUN == 0))
        def _():
            k = (kt - 2 * TURN) // SPLIT
            ssacc[...] += finish(s, k, s_tot)
            pair_a(k).wait_recv()
            ssacc[...] += finish(1 - s, k, s_ag)

        return unused

    steps = U + max(SKEW_L, SKEW_R) * (R - 1) + RUN // 2
    lax.fori_loop(0, steps, step, 0)

    folded = ssacc[...].T
    partial = folded[0:8]
    for q in range(1, LANES // 8):
        partial = partial + folded[q * 8 : (q + 1) * 8]
    ssl[x] = partial

    def p_copy(j, at):
        return remote(ssl.at[at], ssl.at[at], p_send.at[j], p_recv.at[at], {"tp": j})

    each(TP, x, lambda j: p_copy(j, x).start())

    x_copy(pxs, pxr, 0, 0).wait_send()
    remote(s_tot, s_ag, a_send.at[0], a_recv.at[0], sib).wait_send()
    u_x().wait_send()
    pb_x().wait_send()
    carry_a().wait_send()

    @pl.when(jnp.logical_not(last))
    def _():
        carry_l().wait_send()
        l_copy(s_lout, s_lin, 0, 0).wait_send()

    @pl.when(jnp.logical_not(first))
    def _():
        carry_r().wait_send()
        r_copy(s_rout, s_rin, 0, 0).wait_send()

    @pl.when(s == 0)
    def _():
        d_copy().wait_send()
        remote(st0, st0, z_send.at[0], z_recv.at[0], sib).wait_send()

    def told(j, carry):
        tot_copy(j, me).wait_send()
        return carry

    lax.fori_loop(0, me, told, 0)


    each(TP, x, lambda j: p_copy(j, j).wait_recv())
    meansq = jnp.sum(jnp.sum(ssl[...], axis=0), axis=0, keepdims=True) / (C * TP)
    scale_out[...] = jnp.broadcast_to(lax.rsqrt(meansq + 1e-05), scale_out.shape)
    each(TP, x, lambda j: p_copy(j, x).wait_send())


def local(
    prompt_x,
    prompt_b,
    prompt_dt,
    cont_x,
    cont_bc,
    cont_dt,
    decay_rate,
    skip_gain,
    norm_gain,
    steer_vecs,
    mult_table,
    mult_idx,
    behav_idx,
):
    R, TP = lax.axis_size("req"), lax.axis_size("tp")
    H = decay_rate.shape[0]
    tok, C = prompt_x.shape
    Gd, N = prompt_b.shape[1:]
    T = cont_x.shape[1]
    K = C // 2 // WIDTH
    NX = C // 2 // PIECE
    HP = max(H, LANES)
    DEEP = min(K * SPLIT, (R - 1) * max(SKEW_L, SKEW_R) + 2)
    def outside_of(*values):
        return tuple(pltpu.with_memory_space_constraint(v, pltpu.HBM) for v in values)

    args = outside_of(
        prompt_x,
        prompt_b,
        prompt_dt,
        cont_x[0],
        cont_bc[0],
        cont_dt[0],
        decay_rate[None],
        skip_gain[None],
        norm_gain[None],
        steer_vecs,
        mult_table[None],
    ) + (mult_idx, behav_idx)
    vmem, dma = pltpu.VMEM, pltpu.SemaphoreType.DMA
    inside = pl.BlockSpec(memory_space=pltpu.VMEM)
    outside = pl.BlockSpec(memory_space=pl.ANY)
    scalars = pl.BlockSpec(memory_space=pltpu.SMEM)
    part = (K * SPLIT, N // SPLIT, WIDTH)
    carried = (N // 2, H)
    scratch = (
        [
            vmem((tok, H), F32),
            vmem((tok, Gd, N), BF16),
            vmem((1, H), F32),
            vmem((1, H), F32),
            vmem((1, C), F32),
            vmem((1, mult_table.shape[0]), F32),
            vmem((tok, C), BF16),
            vmem((T, C), BF16),
            vmem(cont_bc.shape[1:], BF16),
            vmem((T, H), F32),
            vmem(steer_vecs.shape, F32),
        ]
        + [vmem((NX, tok, PIECE), F32)] * 2
        + [vmem((tok, H), F32)] * 2
        + [vmem((Gd, tok, N), F32)] * 2
        + [vmem((Gd, N, 2 * tok), BF16)]
        + [vmem((2 * tok, HP), F32)]
        + [vmem((T, HP), F32)] * 2
        + [vmem((Gd, T, T + N), BF16), vmem((Gd, N, T), BF16)]
        + [vmem((1, C), F32), vmem((8, C), F32), vmem((8, C), F32)]
        + [vmem((2 * R, 8, H), F32)]
        + [vmem((8, H), F32)] * 2
        + [vmem((2 * K, T, WIDTH), BF16)]
        + [vmem((2 * K, N, WIDTH), F32)]
        + [vmem(part, F32)] * 7
        + [vmem(carried, F32)] * 7
        + [vmem((N, HP), F32), vmem((T, LANES), F32), vmem((TP, 8, T), F32)]
        + [dma((NX + 11,))]
        + [dma((2 * R,))] * 2
        + [dma((3,)), dma((NX + 2,))]
        + [dma((2,)), dma((DEEP + 1,))] * 2
        + [dma((2,)), dma((RING + 1,))]
        + [dma((1,)), dma((2 * K // OCT,))]
        + [dma((1,))] * 2
        + [dma((TP,))] * 2
    )
    mixed, scale = pl.pallas_call(
        functools.partial(kernel, R, TP, K, HP, DEEP),
        out_shape=[jax.ShapeDtypeStruct((T, C), F32), jax.ShapeDtypeStruct((8, T), F32)],
        in_specs=[outside] * 11 + [scalars] * 2,
        out_specs=[inside, inside],
        scratch_shapes=scratch,
        compiler_params=pltpu.CompilerParams(
            collective_id=0, has_side_effects=True, vmem_limit_bytes=40 * 1024 * 1024
        ),
        name="sweep",
    )(*args)
    return (mixed * scale[0][:, None]).astype(BF16)[None]


def solution(mesh):
    return jax.shard_map(
        local,
        mesh=mesh,
        in_specs=(
            P(("parts", "req", "sp"), "tp"),
            P(("parts", "req", "sp"), "tp", None),
            P(("parts", "req", "sp"), "tp"),
            P(("parts", "req"), "sp", "tp"),
            P(("parts", "req"), "sp", None, "tp", None),
            P(("parts", "req"), "sp", "tp"),
            P("tp"),
            P("tp"),
            P("tp"),
            P(None, "tp"),
            P(),
            P(("parts", "req")),
            P(("parts", "req")),
        ),
        out_specs=P(("parts", "req"), "sp", "tp"),
        check_vma=False,
    )
```
